256 devices in a mesh: gx: 32 (over x, z_hi, y), vz: 8 (over z_lo, core).
Axes of the slice: x: 4, y: 4, z: 8 (z_hi: 2, z_lo: 4; z = z_hi * 4 + z_lo), core: 2. Of those that a mesh axis runs over, the one named last changes fastest.
Arguments:
- density: float32 [24, 256, 64, 256], P('vz', 'gx'), may hold values from 0.02 to 2.5, as said below
- shift_depth: int32 [16], replicated, may hold values from -20 to 20, as said below
- sub_cell: float32 [16], replicated, may hold values from 0 to 1
- gravity_kick: float32 [256, 64], P('gx'), may hold values from -0.9 to 0.9
- collision: float32 [256, 64], P('gx'), may hold values from 0.1 to 10
Outputs:
- relaxed: float32 [24, 256, 64, 256], P('vz', 'gx')
The draws below stay inside these ranges and needn't reach their ends.
Inputs may be any that keep to these rules, and one draw needn't show every extreme that they name: `density`: every value is positive. `shift_depth`: some x velocity has 20 and some has -20.
All inputs are finite; a program needn't handle non-finite values.
Results may differ from the reference program's by a relative error of at most 0.00002.
Values sent between devices are 32-bit elements; how exact they have to be, the bound alone decides.
A program may use at most 64 MiB of HBM per device.

```python
import math
import jax
import jax.numpy as jnp
from jax import lax

NVX = 16
NVY = 16
NY = 64
NVXY = 256
NVZ = 24
NX = 256
DMAX = 20


def draw_density(key, part):
    pair = jnp.arange(NVXY, dtype=jnp.int32)
    speed_x = ((pair // NVY).astype(jnp.float32) - (NVX - 1) / 2.0) * (9.0 / NVX)
    speed_y = ((pair % NVY).astype(jnp.float32) - (NVY - 1) / 2.0) * (9.0 / NVY)
    speed_z = (jnp.arange(NVZ, dtype=jnp.float32) - (NVZ - 1) / 2.0) * (9.6 / NVZ)
    deviation_square = speed_x[None, None, None, :] ** 2 + speed_y[None, None, None, :] ** 2 + speed_z[:, None, None, None] ** 2
    shape = (NVZ, NX, NY, NVXY)
    factor = jnp.exp(jax.random.uniform(key, shape, jnp.float32, -0.693, 0.693))
    return (0.02 + factor * jnp.exp(-deviation_square / 2.0)).astype(jnp.float32)


def draw_shift_depth(key, part):
    base = jax.random.randint(key, (NVX,), -DMAX, DMAX + 1, dtype=jnp.int32)
    order = jax.random.permutation(jax.random.fold_in(key, 7), NVX)
    base = base.at[order[0]].set(DMAX)
    base = base.at[order[1]].set(-DMAX)
    return base.astype(jnp.int32)


def level_of(stream_key, dims, shards, low, top_value):
    def one(position, blocks):
        heights = jax.random.uniform(jax.random.fold_in(jax.random.fold_in(stream_key, 6), position), (blocks,), jnp.float32, low / len(shards), top_value / len(shards))
        return jnp.repeat(jnp.exp(heights), dims[position] // blocks).reshape((-1,) + (1,) * (len(dims) - position - 1))

    level = one(*shards[0])
    for cut in shards[1:]:
        level = level * one(*cut)
    return level


def setup_inputs(seed: int = 0) -> dict:
    streams_of = jax.random.split(jax.random.key(seed), 6)
    density = draw_density(jax.random.fold_in(streams_of[5], 71), 0)
    shift_depth = draw_shift_depth(jax.random.fold_in(streams_of[5], 71), 0)
    sub_cell = jnp.clip(jax.random.uniform(streams_of[2], (NVX,), jnp.float32, 0.0, 1.0), 0.0, 1.0)
    gravity_kick = jnp.clip(jax.random.uniform(streams_of[3], (NX, NY), jnp.float32, -0.9, 0.9) * level_of(streams_of[3], (NX, NY), ((0, 32),), -0.4, 0.0), -0.9, 0.9)
    collision = jnp.clip(jnp.exp(math.log(10.0) - 4.6051702 * jax.random.uniform(streams_of[4], (NX, NY), jnp.float32) ** level_of(streams_of[4], (NX, NY), ((0, 32),), -0.2, 0.2)), 0.1, 10.0)
    return dict(density=density, shift_depth=shift_depth, sub_cell=sub_cell, gravity_kick=gravity_kick, collision=collision)


def velocity_axis(count, extent):
    return (jnp.arange(count, dtype=jnp.float32) - (count - 1) / 2.0) * (extent / count)


def reference(density, shift_depth, sub_cell, gravity_kick, collision):
    speed_x = jnp.repeat(velocity_axis(NVX, 9.0), NVY)
    speed_y = jnp.tile(velocity_axis(NVY, 9.0), NVX)
    speed_z = velocity_axis(NVZ, 9.6)
    measure_element = (9.0 / NVX) * (9.0 / NVY) * (9.6 / NVZ)
    depth_each = jnp.repeat(shift_depth, NVY).astype(jnp.int32)
    weight_each = jnp.repeat(sub_cell, NVY)
    columns = jnp.arange(NX, dtype=jnp.int32)[:, None]
    first_rows = jnp.mod(columns - depth_each[None, :], NX).astype(jnp.int32)
    second_rows = jnp.mod(columns - depth_each[None, :] - 1, NX).astype(jnp.int32)
    plane_shape = (NX, NY, NVXY)
    first_full = jnp.broadcast_to(first_rows[:, None, :], plane_shape)
    second_full = jnp.broadcast_to(second_rows[:, None, :], plane_shape)

    def advect(layer):
        near = jnp.take_along_axis(layer, first_full, axis=0)
        far = jnp.take_along_axis(layer, second_full, axis=0)
        return (1.0 - weight_each) * near + weight_each * far

    moved = lax.map(advect, density)
    padded = jnp.pad(moved, ((1, 1), (0, 0), (0, 0), (0, 0)))
    kick = gravity_kick[None, :, :, None]
    weight_accelerated = (1.0 - jnp.abs(kick)) * moved + jnp.maximum(kick, 0.0) * padded[:-2] + jnp.maximum(-kick, 0.0) * padded[2:]
    matter_per_cell = measure_element * jnp.sum(weight_accelerated, axis=(0, 3))
    flow_x = measure_element * jnp.sum(weight_accelerated * speed_x, axis=(0, 3)) / matter_per_cell
    flow_y = measure_element * jnp.sum(weight_accelerated * speed_y, axis=(0, 3)) / matter_per_cell
    flow_z = measure_element * jnp.sum(jnp.sum(weight_accelerated, axis=3) * speed_z[:, None, None], axis=0) / matter_per_cell
    deviation_square = (speed_x - flow_x[None, :, :, None]) ** 2 + (speed_y - flow_y[None, :, :, None]) ** 2 + (speed_z[:, None, None, None] - flow_z[None, :, :, None]) ** 2
    motion_warmth = measure_element * jnp.sum(weight_accelerated * deviation_square, axis=(0, 3)) / (3.0 * matter_per_cell)
    agitation_width = matter_per_cell * (2.0 * jnp.pi * motion_warmth) ** (-1.5)
    equilibrium_profile = agitation_width[None, :, :, None] * jnp.exp(-deviation_square / (2.0 * motion_warmth[None, :, :, None]))
    rate = collision[None, :, :, None]
    return (weight_accelerated + rate * equilibrium_profile) / (1.0 + rate)
```

```python
import functools
import math

import jax
import jax.numpy as jnp
from jax import lax
from jax.experimental import pallas as pl
from jax.experimental.pallas import tpu as pltpu
from jax.sharding import Mesh
from jax.sharding import PartitionSpec as P

AXES = ("x", "zh", "y", "zl", "core")
VZ = ("zl", "core")
GX = ("x", "zh", "y")
MESH = pl.DeviceIdType.MESH
HIGH = lax.Precision.HIGHEST

NVX = 16
COLS = 8
WIDE = 32
ROWS = 64
QUARTER = 16
PLANES = 3
TOTAL_VZ = 24
TR = 8
TILES = QUARTER // TR
CHUNKS = [(p, t) for p in (0, 2, 1) for t in range(TILES)]
N = len(CHUNKS)
FULL = 42

LANES = (slice(0, 128), slice(128, 256))
STEP_XY = 9.0 / 16
STEP_Z = 9.6 / TOTAL_VZ
CELL = STEP_XY * STEP_XY * STEP_Z


def kernel(
    cap,
    depth,
    sub,
    kick,
    rate,
    dens,
    out,
    *scratch,
):
    scratch = list(scratch)
    take = lambda k: [scratch.pop(0) for _ in range(k)]
    block, packed, lists, chosen, moved = (take(N) for _ in range(5))
    planes, kick_wide, plane_sums, part, parts, coef, wide, unit_col, unit_half, unit_turn = take(10)
    y1_own, y1_out, y1_in, z_out, z_in, x_out, x_in = take(7)
    y2_own, y2_out, y2_in, halo_out, halo_in, sum_out, sum_in = take(7)

    x, zh, y = (lax.axis_index(a) for a in GX)
    zl, core = (lax.axis_index(a) for a in VZ)
    nx = lax.axis_size("x")
    slab = zl * 2 + core
    slabs = lax.axis_size("zl") * 2

    def slab_device(v):
        return {"zl": v // 2, "core": v % 2}

    barrier = pltpu.get_barrier_semaphore()
    friends = [{"y": (y + k) % 4} for k in (1, 2, 3)]
    friends += [{"zh": 1 - zh}, {"x": (x + 1) % nx}, {"x": (x + nx - 1) % nx}]
    friends += [slab_device((slab + k) % slabs) for k in range(1, 8)]
    for friend in friends:
        pl.semaphore_signal(barrier, inc=1, device_id=friend, device_id_type=MESH)

    own = []
    for c, (p, t) in enumerate(CHUNKS):
        rows = pl.ds(y * QUARTER + t * TR, TR)
        own.append(
            [
                pltpu.make_async_copy(
                    dens.at[p, :, rows, LANES[h]], block[c].at[h, pl.ds(y * COLS, COLS)], y1_own.at[c, h]
                )
                for h in range(2)
            ]
        )
        for copy in own[c]:
            copy.start()
    pl.semaphore_wait(barrier, len(friends))

    def remote(src, dst, send, recv, device):
        return pltpu.make_async_remote_copy(
            src_ref=src, dst_ref=dst, send_sem=send, recv_sem=recv, device_id=device, device_id_type=MESH
        )

    y1 = []
    for c, (p, t) in enumerate(CHUNKS):
        group = []
        for k in range(3):
            to = (y + k + 1) % 4
            rows = pl.ds(to * QUARTER + t * TR, TR)
            for h in range(2):
                group.append(
                    remote(
                        dens.at[p, :, rows, LANES[h]],
                        block[c].at[h, pl.ds(y * COLS, COLS)],
                        y1_out.at[c, 2 * k + h],
                        y1_in.at[c, 2 * k + h],
                        {"y": to},
                    )
                )
                group[-1].start()
        y1.append(group)

    def next_unit(u, state):
        i, j = state
        d = depth[i]
        count = jnp.where(d >= 0, d + 1, -d)
        col = jnp.where(d >= 0, WIDE - 1 - d + j, j)
        unit_col[u] = jnp.minimum(jnp.maximum(col, 0), WIDE - 1)
        unit_half[u] = i >> 3
        unit_turn[u] = ((u - i) & 7) * 16
        last = j + 1 >= count
        return jnp.where(last, jnp.minimum(i + 1, NVX - 1), i), jnp.where(last, 0, j + 1)

    lax.fori_loop(0, cap * 8, next_unit, (jnp.int32(0), jnp.int32(0)))

    depths = [depth[i] for i in range(NVX)]
    first, start = [], jnp.int32(0)
    for d in depths:
        first.append(start + jnp.where(d >= 0, 1, -d - WIDE))
        start = start + jnp.where(d >= 0, d + 1, -d)
    side_rows = [jnp.where(d >= 0, 0, cap) for d in depths]

    lane_group = lax.broadcasted_iota(jnp.int32, (TR, 128), 1) >> 4

    def by_group(values, h):
        acc = jnp.full((TR, 128), values[h * 8])
        for s in range(1, 8):
            acc = jnp.where(lane_group == s, values[h * 8 + s], acc)
        return acc

    lane_depth = [by_group(depths, h) for h in range(2)]
    lane_far = [by_group([sub[i] for i in range(NVX)], h) for h in range(2)]

    pair = lax.broadcasted_iota(jnp.int32, (8, 256), 1)
    vx_of = ((pair >> 4).astype(jnp.float32) - 7.5) * STEP_XY
    vy_of = ((pair & 15).astype(jnp.float32) - 7.5) * STEP_XY
    which = lax.broadcasted_iota(jnp.int32, (8, 256), 0)
    weights = jnp.where(
        which == 0,
        1.0,
        jnp.where(which == 1, vx_of, jnp.where(which == 2, vy_of, jnp.where(which == 3, vx_of**2 + vy_of**2, 0.0))),
    )

    def spread(values, c):
        pick = (lax.broadcasted_iota(jnp.int32, (8, 128), 0) == c).astype(jnp.float32)
        return lax.dot_general(
            values, pick, (((0,), (0,)), ((), ())), precision=HIGH, preferred_element_type=jnp.float32
        )

    def widen_kick(c, _):
        kick_wide[c] = spread(kick[...], c)
        return 0

    lax.fori_loop(0, COLS, widen_kick, 0)

    @pl.when(slab == 0)
    def _():
        planes[0] = jnp.zeros((COLS, ROWS, 256), jnp.float32)

    @pl.when(slab == slabs - 1)
    def _():
        planes[4] = jnp.zeros((COLS, ROWS, 256), jnp.float32)

    z_copies, x_copies, y2, y2_self = {}, {}, {}, {}

    def stage_pack(c):
        for copy in own[c]:
            copy.wait()
        for copy in y1[c]:
            copy.wait_recv()

        def one_row(r, _):
            acc = None
            for s in range(8):
                u = r * 8 + s
                piece = pltpu.roll(block[c][unit_half[u], unit_col[u]], unit_turn[u], 1)
                acc = piece if s == 0 else jnp.where(lane_group == s, piece, acc)
            packed[c][r] = acc
            return 0

        lax.fori_loop(0, cap, one_row, 0)
        z_copies[c] = remote(
            packed[c], lists[c].at[pl.ds(zh * cap, cap)], z_out.at[c], z_in.at[c], {"zh": 1 - zh}
        )
        z_copies[c].start()

        def one_col(n, _):
            for h in range(2):
                acc = None
                for s in range(8):
                    col = jnp.minimum(jnp.maximum(n - 1 - depths[h * 8 + s], 0), WIDE - 1)
                    piece = block[c][h, col]
                    acc = piece if s == 0 else jnp.where(lane_group == s, piece, acc)
                chosen[c][n, :, h * 128 : h * 128 + 128] = acc
            return 0

        lax.fori_loop(0, WIDE + 1, one_col, 0)

    def stage_forward(c):
        z_copies[c].wait_recv()
        x_copies[c] = remote(
            lists[c].at[pl.ds((1 - zh) * cap, cap)],
            lists[c].at[pl.ds(zh * cap, cap)],
            x_out.at[c],
            x_in.at[c],
            {"x": (x + 1 - 2 * zh + nx) % nx},
        )
        x_copies[c].start()

    def stage_merge(c):
        x_copies[c].wait_recv()
        p, t = CHUNKS[c]

        def column(n):
            got = []
            for h in range(2):
                acc = None
                for s in range(8):
                    i = h * 8 + s
                    u = jnp.minimum(jnp.maximum(first[i] + n - 1, 0), cap * 8 - 1)
                    piece = pltpu.roll(lists[c][(u >> 3) + side_rows[i]], ((s - u) & 7) * 16, 1)
                    acc = piece if s == 0 else jnp.where(lane_group == s, piece, acc)
                from_col = n - 1 - lane_depth[h]
                local = jnp.logical_and(from_col >= 0, from_col < WIDE)
                got.append(jnp.where(local, chosen[c][n, :, h * 128 : h * 128 + 128], acc))
            return got

        def one_col(n, before):
            now = column(n)
            for h in range(2):
                moved[c][n - 1, :, h * 128 : h * 128 + 128] = (1.0 - lane_far[h]) * now[h] + lane_far[h] * before[h]
            return tuple(now)

        lax.fori_loop(1, WIDE + 1, one_col, tuple(column(0)))
        here = planes.at[p + 1, :, pl.ds(y * QUARTER + t * TR, TR), :]
        y2[c] = []
        for k in range(3):
            to = (y + k + 1) % 4
            y2[c].append(
                remote(moved[c].at[pl.ds(to * COLS, COLS)], here, y2_out.at[c, k], y2_in.at[c, k], {"y": to})
            )
            y2[c][k].start()
        y2_self[c] = pltpu.make_async_copy(moved[c].at[pl.ds(y * COLS, COLS)], here, y2_own.at[c])
        y2_self[c].start()

    down = remote(planes.at[1], planes.at[4], halo_out.at[0], halo_in.at[0], slab_device((slab + slabs - 1) % slabs))
    up = remote(planes.at[3], planes.at[0], halo_out.at[1], halo_in.at[1], slab_device((slab + 1) % slabs))

    def stage_plane(p):
        for c, (q, _) in enumerate(CHUNKS):
            if q == p:
                y2_self[c].wait()
                for k in range(3):
                    y2[c][k].wait_recv()
        if p == 0:
            pl.when(slab > 0)(down.start)
        if p == 2:
            pl.when(slab < slabs - 1)(up.start)

        def one_col(c, _):
            plane_sums[p, c] = lax.dot_general(
                weights,
                planes[p + 1, c],
                (((1,), (1,)), ((), ())),
                precision=HIGH,
                preferred_element_type=jnp.float32,
            )
            return 0

        lax.fori_loop(0, COLS, one_col, 0)

    for name, c in ORDER:
        {"A": stage_pack, "B": stage_forward, "C": stage_merge, "D": stage_plane}[name](c)

    a = kick[...]
    lift, drop, stay = jnp.maximum(a, 0.0), jnp.maximum(-a, 0.0), 1.0 - jnp.abs(a)
    totals = [jnp.zeros((COLS, ROWS), jnp.float32) for _ in range(5)]
    for p in range(PLANES):
        level = slab * PLANES + p
        up_on = jnp.where(level + 1 < TOTAL_VZ, lift, 0.0)
        down_on = jnp.where(level >= 1, drop, 0.0)
        vz = (level.astype(jnp.float32) - 11.5) * STEP_Z
        above = ((level + 1).astype(jnp.float32) - 11.5) * STEP_Z
        below = ((level - 1).astype(jnp.float32) - 11.5) * STEP_Z
        kept = stay + up_on + down_on
        lean = stay * vz + up_on * above + down_on * below
        heat = stay * (vz * vz) + up_on * (above * above) + down_on * (below * below)
        n0, n1, n2, n3 = (plane_sums[p, :, j, :] for j in range(4))
        for j, term in enumerate((n0 * kept, n1 * kept, n2 * kept, n0 * lean, n3 * kept + n0 * heat)):
            totals[j] = totals[j] + term
    for j in range(5):
        part[j, :, 0:ROWS] = totals[j]

    shares = []
    for k in range(7):
        shares.append(remote(part, parts.at[k], sum_out.at[k], sum_in.at[k], slab_device((slab + k + 1) % slabs)))
        shares[k].start()
    for k in range(7):
        shares[k].wait_recv()
    for j in range(5):
        for k in range(7):
            totals[j] = totals[j] + parts[k, j, :, 0:ROWS]

    mass = CELL * totals[0]
    flow_x = CELL * totals[1] / mass
    flow_y = CELL * totals[2] / mass
    flow_z = CELL * totals[3] / mass
    warm = (CELL * totals[4] - mass * (flow_x**2 + flow_y**2 + flow_z**2)) / (3.0 * mass)
    r = rate[...]
    share = 1.0 / (1.0 + r)
    two_pi_t = (2.0 * math.pi) * warm
    top = mass / (two_pi_t * jnp.sqrt(two_pi_t))
    for j, value in enumerate((share, r * share * top, -0.5 / warm, flow_x, flow_y, flow_z)):
        coef[j] = value

    pl.when(slab > 0)(up.wait_recv)
    pl.when(slab < slabs - 1)(down.wait_recv)

    def finish(c, _):
        for j in range(6):
            wide[j] = spread(coef[j], c)

        def rows_of(n, _):
            rows = pl.ds(pl.multiple_of(n * 8, 8), 8)
            keep, gain, cool, ux, uy, uz = (wide[j, rows, :] for j in range(6))
            a = kick_wide[c, rows, :]
            lift, drop, stay = jnp.maximum(a, 0.0), jnp.maximum(-a, 0.0), 1.0 - jnp.abs(a)
            for h in range(2):
                lanes = slice(h * 128, h * 128 + 128)
                flat = (vx_of[:, lanes] - ux) ** 2 + (vy_of[:, lanes] - uy) ** 2
                f = [planes[q, c, rows, lanes] for q in range(5)]
                for p in range(PLANES):
                    vz = ((slab * PLANES + p).astype(jnp.float32) - 11.5) * STEP_Z
                    bell = jnp.exp(cool * (flat + (vz - uz) ** 2))
                    kicked = stay * f[p + 1] + lift * f[p] + drop * f[p + 2]
                    out[p, c, rows, lanes] = keep * kicked + gain * bell
            return 0

        lax.fori_loop(0, ROWS // 8, rows_of, 0)
        return 0

    lax.fori_loop(0, COLS, finish, 0)

    pl.when(slab > 0)(down.wait_send)
    pl.when(slab < slabs - 1)(up.wait_send)
    for k in range(7):
        shares[k].wait_send()
    for c in range(N):
        z_copies[c].wait_send()
        x_copies[c].wait_send()
        for copy in y1[c] + y2[c]:
            copy.wait_send()


ORDER = (
    ("A", 0), ("A", 1), ("A", 2), ("B", 0), ("A", 3), ("C", 0), ("B", 1), ("A", 4), ("A", 5), ("C", 1), ("B", 2),
    ("C", 2), ("D", 0), ("B", 3), ("C", 3), ("B", 4), ("D", 2), ("C", 4), ("B", 5), ("C", 5), ("D", 1),
)


def step(cap, collective_id, density, shift_depth, sub_cell, gravity_kick, collision):
    f32 = jnp.float32
    vmem = pl.BlockSpec(memory_space=pltpu.VMEM)
    smem = pl.BlockSpec(memory_space=pltpu.SMEM)
    dma = pltpu.SemaphoreType.DMA
    return pl.pallas_call(
        functools.partial(kernel, cap),
        out_shape=jax.ShapeDtypeStruct((PLANES, COLS, ROWS, 256), f32),
        in_specs=[smem, smem, vmem, vmem, pl.BlockSpec(memory_space=pl.ANY)],
        out_specs=vmem,
        scratch_shapes=[pltpu.VMEM((2, WIDE, TR, 128), f32)] * N
        + [pltpu.VMEM((cap, TR, 128), f32)] * N
        + [pltpu.VMEM((2 * cap, TR, 128), f32)] * N
        + [pltpu.VMEM((WIDE + 1, TR, 256), f32)] * N
        + [pltpu.VMEM((WIDE, TR, 256), f32)] * N
        + [
            pltpu.VMEM((5, COLS, ROWS, 256), f32),
            pltpu.VMEM((COLS, ROWS, 128), f32),
            pltpu.VMEM((PLANES, COLS, 8, ROWS), f32),
            pltpu.VMEM((5, COLS, 128), f32),
            pltpu.VMEM((7, 5, COLS, 128), f32),
            pltpu.VMEM((6, COLS, ROWS), f32),
            pltpu.VMEM((6, ROWS, 128), f32),
            pltpu.SMEM((cap * 8,), jnp.int32),
            pltpu.SMEM((cap * 8,), jnp.int32),
            pltpu.SMEM((cap * 8,), jnp.int32),
            dma((N, 2)),
            dma((N, 6)),
            dma((N, 6)),
            dma((N,)),
            dma((N,)),
            dma((N,)),
            dma((N,)),
            dma((N,)),
            dma((N, 3)),
            dma((N, 3)),
            dma((2,)),
            dma((2,)),
            dma((7,)),
            dma((7,)),
        ],
        compiler_params=pltpu.CompilerParams(collective_id=collective_id, has_side_effects=True),
    )(shift_depth, sub_cell, gravity_kick, collision, density)


def per_device(density, shift_depth, sub_cell, gravity_kick, collision):
    return step(FULL, 1, density, shift_depth, sub_cell, gravity_kick, collision)


def solution(mesh):
    torus = Mesh(mesh.devices.reshape(mesh.shape["gx"] // 8, 2, 4, 4, 2), AXES)
    return jax.shard_map(
        per_device,
        mesh=torus,
        in_specs=(P(VZ, GX, None, None), P(), P(), P(GX, None), P(GX, None)),
        out_specs=P(VZ, GX, None, None),
        check_vma=False,
    )
```

```python
import functools
import math

import jax
import jax.numpy as jnp
from jax import lax
from jax.experimental import pallas as pl
from jax.experimental.pallas import tpu as pltpu
from jax.sharding import Mesh
from jax.sharding import PartitionSpec as P

AXES = ("x", "zh", "y", "zl", "core")
VZ = ("zl", "core")
GX = ("x", "zh", "y")
MESH = pl.DeviceIdType.MESH
HIGH = lax.Precision.HIGHEST

NVX = 16
COLS = 8
WIDE = 32
ROWS = 64
QUARTER = 16
PLANES = 3
TOTAL_VZ = 24
TR = 8
TILES = QUARTER // TR
CHUNKS = [(p, t) for p in (0, 2, 1) for t in range(TILES)]
N = len(CHUNKS)
FULL = 42
REACH = 21
SPAN = WIDE + 2 * REACH

LANES = (slice(0, 128), slice(128, 256))
STEP_XY = 9.0 / 16
STEP_Z = 9.6 / TOTAL_VZ
CELL = STEP_XY * STEP_XY * STEP_Z


def kernel(
    cap,
    depth,
    sub,
    kick,
    rate,
    dens,
    out,
    *scratch,
):
    scratch = list(scratch)
    take = lambda k: [scratch.pop(0) for _ in range(k)]
    block, packed, lists, chosen, moved = (take(N) for _ in range(5))
    planes, kick_wide, plane_sums, part, parts, coef, wide, order, local, remote_cols, mixed = take(11)
    y1_own, y1_out, y1_in, z_out, z_in, x_out, x_in = take(7)
    y2_own, y2_out, y2_in, halo_out, halo_in, sum_out, sum_in = take(7)

    x, zh, y = (lax.axis_index(a) for a in GX)
    zl, core = (lax.axis_index(a) for a in VZ)
    nx = lax.axis_size("x")
    slab = zl * 2 + core
    slabs = lax.axis_size("zl") * 2

    def slab_device(v):
        return {"zl": v // 2, "core": v % 2}

    barrier = pltpu.get_barrier_semaphore()
    friends = [{"y": (y + k) % 4} for k in (1, 2, 3)]
    friends += [{"zh": 1 - zh}, {"x": (x + 1) % nx}, {"x": (x + nx - 1) % nx}]
    friends += [slab_device((slab + k) % slabs) for k in range(1, 8)]
    for friend in friends:
        pl.semaphore_signal(barrier, inc=1, device_id=friend, device_id_type=MESH)

    own = []
    for c, (p, t) in enumerate(CHUNKS):
        rows = pl.ds(y * QUARTER + t * TR, TR)
        own.append(pltpu.make_async_copy(dens.at[p, :, rows, :], block[c].at[pl.ds(y * COLS, COLS)], y1_own.at[c]))
        own[c].start()
    pl.semaphore_wait(barrier, len(friends))

    def remote(src, dst, send, recv, device):
        return pltpu.make_async_remote_copy(
            src_ref=src, dst_ref=dst, send_sem=send, recv_sem=recv, device_id=device, device_id_type=MESH
        )

    y1 = []
    for c, (p, t) in enumerate(CHUNKS):
        group = []
        for k in range(3):
            to = (y + k + 1) % 4
            rows = pl.ds(to * QUARTER + t * TR, TR)
            group.append(
                remote(
                    dens.at[p, :, rows, :],
                    block[c].at[pl.ds(y * COLS, COLS)],
                    y1_out.at[c, k],
                    y1_in.at[c, k],
                    {"y": to},
                )
            )
            group[-1].start()
        y1.append(group)

    depths = [depth[i] for i in range(NVX)]
    counts = [jnp.where(d >= 0, d + 1, -d) for d in depths]
    ranks = [jnp.int32(0)] * NVX
    for i in range(NVX):
        for j in range(i):
            behind = (counts[i] <= counts[j]).astype(jnp.int32)
            ranks[i] = ranks[i] + behind
            ranks[j] = ranks[j] + 1 - behind
    places = [jnp.where(r < 8, r, 23 - r) for r in ranks]

    def at_place(values, q):
        acc = values[0]
        for i in range(1, NVX):
            acc = jnp.where(places[i] == q, values[i], acc)
        return acc

    depths = [at_place(depths, q) for q in range(NVX)]
    far = [at_place([sub[i] for i in range(NVX)], q) for q in range(NVX)]
    counts = [jnp.where(d >= 0, d + 1, -d) for d in depths]
    edge = [REACH + jnp.where(d >= 0, WIDE - 1 - d, 0) for d in depths]
    upper = edge[:8]
    lower = [SPAN + edge[8 + s] - counts[s] for s in range(8)]
    lists_at = [jnp.where(d >= 0, 0, cap - d - REACH) for d in depths]
    for s in range(8):
        lists_at[8 + s] = lists_at[8 + s] + counts[s]

    to_lane = lax.broadcasted_iota(jnp.int32, (16, 256), 1)
    to_sub = lax.broadcasted_iota(jnp.int32, (16, 256), 0)
    for i in range(NVX):
        order[i * 16 : i * 16 + 16, :] = (to_lane == places[i] * 16 + to_sub).astype(jnp.bfloat16)

    def permute(values, back):
        total = None
        for _ in range(3):
            piece = values.astype(jnp.bfloat16)
            values = values - piece.astype(jnp.float32)
            term = lax.dot_general(
                piece, order[...], (((1,), (1 if back else 0,)), ((), ())), preferred_element_type=jnp.float32
            )
            total = term if total is None else total + term
        return total

    lane_group = lax.broadcasted_iota(jnp.int32, (TR, 128), 1) >> 4

    def by_group(values, h):
        acc = jnp.full((TR, 128), values[h * 8])
        for s in range(1, 8):
            acc = jnp.where(lane_group == s, values[h * 8 + s], acc)
        return acc

    lane_depth = [by_group(depths, h) for h in range(2)]
    lane_far = [by_group(far, h) for h in range(2)]

    pair = lax.broadcasted_iota(jnp.int32, (8, 256), 1)
    vx_of = ((pair >> 4).astype(jnp.float32) - 7.5) * STEP_XY
    vy_of = ((pair & 15).astype(jnp.float32) - 7.5) * STEP_XY
    which = lax.broadcasted_iota(jnp.int32, (8, 256), 0)
    weights = jnp.where(
        which == 0,
        1.0,
        jnp.where(which == 1, vx_of, jnp.where(which == 2, vy_of, jnp.where(which == 3, vx_of**2 + vy_of**2, 0.0))),
    )

    def spread(values, c):
        pick = (lax.broadcasted_iota(jnp.int32, (8, 128), 0) == c).astype(jnp.float32)
        return lax.dot_general(
            values, pick, (((0,), (0,)), ((), ())), precision=HIGH, preferred_element_type=jnp.float32
        )

    def widen_kick(c, _):
        kick_wide[c] = spread(kick[...], c)
        return 0

    lax.fori_loop(0, COLS, widen_kick, 0)

    @pl.when(slab == 0)
    def _():
        planes[0] = jnp.zeros((COLS, ROWS, 256), jnp.float32)

    @pl.when(slab == slabs - 1)
    def _():
        planes[4] = jnp.zeros((COLS, ROWS, 256), jnp.float32)

    z_copies, x_copies, y2, y2_self = {}, {}, {}, {}

    def stage_pack(c):
        own[c].wait()
        for copy in y1[c]:
            copy.wait_recv()

        for b in range(2):
            cols = slice(b * 16, b * 16 + 16)
            lined = permute(block[c][cols].reshape(16 * TR, 256), False)
            for h in range(2):
                at = h * SPAN + REACH + b * 16
                local[at : at + 16] = lined[:, LANES[h]].reshape(16, TR, 128)

        def one_row(r, _):
            acc = None
            for s in range(8):
                piece = local[r + jnp.where(r < counts[s], upper[s], lower[s])]
                acc = piece if s == 0 else jnp.where(lane_group == s, piece, acc)
            packed[c][r] = acc
            return 0

        lax.fori_loop(0, cap, one_row, 0)
        z_copies[c] = remote(
            packed[c], lists[c].at[pl.ds(zh * cap, cap)], z_out.at[c], z_in.at[c], {"zh": 1 - zh}
        )
        z_copies[c].start()

        def one_col(n, _):
            for h in range(2):
                acc = None
                for s in range(8):
                    piece = local[n + (h * SPAN + REACH - 1 - depths[h * 8 + s])]
                    acc = piece if s == 0 else jnp.where(lane_group == s, piece, acc)
                chosen[c][n, :, LANES[h]] = acc
            return 0

        lax.fori_loop(0, WIDE + 1, one_col, 0)

    def stage_forward(c):
        z_copies[c].wait_recv()
        x_copies[c] = remote(
            lists[c].at[pl.ds((1 - zh) * cap, cap)],
            lists[c].at[pl.ds(zh * cap, cap)],
            x_out.at[c],
            x_in.at[c],
            {"x": (x + 1 - 2 * zh + nx) % nx},
        )
        x_copies[c].start()

    def stage_merge(c):
        x_copies[c].wait_recv()
        p, t = CHUNKS[c]

        def one_remote(j, _):
            for h in range(2):
                acc = None
                for s in range(8):
                    piece = lists[c][j + lists_at[h * 8 + s]]
                    acc = piece if s == 0 else jnp.where(lane_group == s, piece, acc)
                remote_cols[j + 12, :, LANES[h]] = acc
            return 0

        lax.fori_loop(0, REACH, one_remote, 0)

        def column(n):
            got = []
            for h in range(2):
                from_col = n - 1 - lane_depth[h]
                inside = jnp.logical_and(from_col >= 0, from_col < WIDE)
                beyond = jnp.where(
                    lane_depth[h] >= 0, remote_cols[n + 12, :, LANES[h]], remote_cols[n, :, LANES[h]]
                )
                got.append(jnp.where(inside, chosen[c][n, :, LANES[h]], beyond))
            return got

        def one_col(n, before):
            now = column(n)
            for h in range(2):
                mixed[n - 1, :, LANES[h]] = (1.0 - lane_far[h]) * now[h] + lane_far[h] * before[h]
            return tuple(now)

        lax.fori_loop(1, WIDE + 1, one_col, tuple(column(0)))
        for b in range(2):
            cols = slice(b * 16, b * 16 + 16)
            moved[c][cols] = permute(mixed[cols].reshape(16 * TR, 256), True).reshape(16, TR, 256)
        here = planes.at[p + 1, :, pl.ds(y * QUARTER + t * TR, TR), :]
        y2[c] = []
        for k in range(3):
            to = (y + k + 1) % 4
            y2[c].append(
                remote(moved[c].at[pl.ds(to * COLS, COLS)], here, y2_out.at[c, k], y2_in.at[c, k], {"y": to})
            )
            y2[c][k].start()
        y2_self[c] = pltpu.make_async_copy(moved[c].at[pl.ds(y * COLS, COLS)], here, y2_own.at[c])
        y2_self[c].start()

    down = remote(planes.at[1], planes.at[4], halo_out.at[0], halo_in.at[0], slab_device((slab + slabs - 1) % slabs))
    up = remote(planes.at[3], planes.at[0], halo_out.at[1], halo_in.at[1], slab_device((slab + 1) % slabs))

    def stage_plane(p):
        for c, (q, _) in enumerate(CHUNKS):
            if q == p:
                y2_self[c].wait()
                for k in range(3):
                    y2[c][k].wait_recv()
        if p == 0:
            pl.when(slab > 0)(down.start)
        if p == 2:
            pl.when(slab < slabs - 1)(up.start)

        def one_col(c, _):
            plane_sums[p, c] = lax.dot_general(
                weights,
                planes[p + 1, c],
                (((1,), (1,)), ((), ())),
                precision=HIGH,
                preferred_element_type=jnp.float32,
            )
            return 0

        lax.fori_loop(0, COLS, one_col, 0)

    for name, c in ORDER:
        {"A": stage_pack, "B": stage_forward, "C": stage_merge, "D": stage_plane}[name](c)

    a = kick[...]
    lift, drop, stay = jnp.maximum(a, 0.0), jnp.maximum(-a, 0.0), 1.0 - jnp.abs(a)
    totals = [jnp.zeros((COLS, ROWS), jnp.float32) for _ in range(5)]
    for p in range(PLANES):
        level = slab * PLANES + p
        up_on = jnp.where(level + 1 < TOTAL_VZ, lift, 0.0)
        down_on = jnp.where(level >= 1, drop, 0.0)
        vz = (level.astype(jnp.float32) - 11.5) * STEP_Z
        above = ((level + 1).astype(jnp.float32) - 11.5) * STEP_Z
        below = ((level - 1).astype(jnp.float32) - 11.5) * STEP_Z
        kept = stay + up_on + down_on
        lean = stay * vz + up_on * above + down_on * below
        heat = stay * (vz * vz) + up_on * (above * above) + down_on * (below * below)
        n0, n1, n2, n3 = (plane_sums[p, :, j, :] for j in range(4))
        for j, term in enumerate((n0 * kept, n1 * kept, n2 * kept, n0 * lean, n3 * kept + n0 * heat)):
            totals[j] = totals[j] + term
    for j in range(5):
        part[j, :, 0:ROWS] = totals[j]

    shares = []
    for k in range(7):
        shares.append(remote(part, parts.at[k], sum_out.at[k], sum_in.at[k], slab_device((slab + k + 1) % slabs)))
        shares[k].start()
    for k in range(7):
        shares[k].wait_recv()
    for j in range(5):
        for k in range(7):
            totals[j] = totals[j] + parts[k, j, :, 0:ROWS]

    mass = CELL * totals[0]
    flow_x = CELL * totals[1] / mass
    flow_y = CELL * totals[2] / mass
    flow_z = CELL * totals[3] / mass
    warm = (CELL * totals[4] - mass * (flow_x**2 + flow_y**2 + flow_z**2)) / (3.0 * mass)
    r = rate[...]
    share = 1.0 / (1.0 + r)
    two_pi_t = (2.0 * math.pi) * warm
    top = mass / (two_pi_t * jnp.sqrt(two_pi_t))
    for j, value in enumerate((share, r * share * top, -0.5 / warm, flow_x, flow_y, flow_z)):
        coef[j] = value

    pl.when(slab > 0)(up.wait_recv)
    pl.when(slab < slabs - 1)(down.wait_recv)

    def finish(c, _):
        for j in range(6):
            wide[j] = spread(coef[j], c)

        def rows_of(n, _):
            rows = pl.ds(pl.multiple_of(n * 8, 8), 8)
            keep, gain, cool, ux, uy, uz = (wide[j, rows, :] for j in range(6))
            a = kick_wide[c, rows, :]
            lift, drop, stay = jnp.maximum(a, 0.0), jnp.maximum(-a, 0.0), 1.0 - jnp.abs(a)
            for h in range(2):
                lanes = slice(h * 128, h * 128 + 128)
                flat = (vx_of[:, lanes] - ux) ** 2 + (vy_of[:, lanes] - uy) ** 2
                f = [planes[q, c, rows, lanes] for q in range(5)]
                for p in range(PLANES):
                    vz = ((slab * PLANES + p).astype(jnp.float32) - 11.5) * STEP_Z
                    bell = jnp.exp(cool * (flat + (vz - uz) ** 2))
                    kicked = stay * f[p + 1] + lift * f[p] + drop * f[p + 2]
                    out[p, c, rows, lanes] = keep * kicked + gain * bell
            return 0

        lax.fori_loop(0, ROWS // 8, rows_of, 0)
        return 0

    lax.fori_loop(0, COLS, finish, 0)

    pl.when(slab > 0)(down.wait_send)
    pl.when(slab < slabs - 1)(up.wait_send)
    for k in range(7):
        shares[k].wait_send()
    for c in range(N):
        z_copies[c].wait_send()
        x_copies[c].wait_send()
        for copy in y1[c] + y2[c]:
            copy.wait_send()


ORDER = (
    ("A", 0), ("A", 1), ("A", 2), ("B", 0), ("A", 3), ("C", 0), ("B", 1), ("A", 4), ("A", 5), ("C", 1), ("B", 2),
    ("C", 2), ("D", 0), ("B", 3), ("C", 3), ("B", 4), ("D", 2), ("C", 4), ("B", 5), ("C", 5), ("D", 1),
)


def step(cap, collective_id, density, shift_depth, sub_cell, gravity_kick, collision):
    f32 = jnp.float32
    vmem = pl.BlockSpec(memory_space=pltpu.VMEM)
    smem = pl.BlockSpec(memory_space=pltpu.SMEM)
    dma = pltpu.SemaphoreType.DMA
    return pl.pallas_call(
        functools.partial(kernel, cap),
        out_shape=jax.ShapeDtypeStruct((PLANES, COLS, ROWS, 256), f32),
        in_specs=[smem, smem, vmem, vmem, pl.BlockSpec(memory_space=pl.ANY)],
        out_specs=vmem,
        scratch_shapes=[pltpu.VMEM((WIDE, TR, 256), f32)] * N
        + [pltpu.VMEM((cap, TR, 128), f32)] * N
        + [pltpu.VMEM((max(2 * cap, cap + 2 * REACH), TR, 128), f32)] * N
        + [pltpu.VMEM((WIDE + 1, TR, 256), f32)] * N
        + [pltpu.VMEM((WIDE, TR, 256), f32)] * N
        + [
            pltpu.VMEM((5, COLS, ROWS, 256), f32),
            pltpu.VMEM((COLS, ROWS, 128), f32),
            pltpu.VMEM((PLANES, COLS, 8, ROWS), f32),
            pltpu.VMEM((5, COLS, 128), f32),
            pltpu.VMEM((7, 5, COLS, 128), f32),
            pltpu.VMEM((6, COLS, ROWS), f32),
            pltpu.VMEM((6, ROWS, 128), f32),
            pltpu.VMEM((256, 256), jnp.bfloat16),
            pltpu.VMEM((2 * SPAN + 2 * REACH, TR, 128), f32),
            pltpu.VMEM((REACH + 24, TR, 256), f32),
            pltpu.VMEM((WIDE, TR, 256), f32),
            dma((N,)),
            dma((N, 3)),
            dma((N, 3)),
            dma((N,)),
            dma((N,)),
            dma((N,)),
            dma((N,)),
            dma((N,)),
            dma((N, 3)),
            dma((N, 3)),
            dma((2,)),
            dma((2,)),
            dma((7,)),
            dma((7,)),
        ],
        compiler_params=pltpu.CompilerParams(collective_id=collective_id, has_side_effects=True),
    )(shift_depth, sub_cell, gravity_kick, collision, density)


def per_device(density, shift_depth, sub_cell, gravity_kick, collision):
    return step(FULL, 1, density, shift_depth, sub_cell, gravity_kick, collision)


def solution(mesh):
    torus = Mesh(mesh.devices.reshape(mesh.shape["gx"] // 8, 2, 4, 4, 2), AXES)
    return jax.shard_map(
        per_device,
        mesh=torus,
        in_specs=(P(VZ, GX, None, None), P(), P(), P(GX, None), P(GX, None)),
        out_specs=P(VZ, GX, None, None),
        check_vma=False,
    )
```

```python
import functools
import math

import jax
import jax.numpy as jnp
from jax import lax
from jax.experimental import pallas as pl
from jax.experimental.pallas import tpu as pltpu
from jax.sharding import Mesh
from jax.sharding import PartitionSpec as P

AXES = ("x", "zh", "y", "zl", "core")
VZ = ("zl", "core")
GX = ("x", "zh", "y")
MESH = pl.DeviceIdType.MESH
HIGH = lax.Precision.HIGHEST

NVX = 16
COLS = 8
WIDE = 32
ROWS = 64
QUARTER = 16
PLANES = 3
TOTAL_VZ = 24
TR = 8
TILES = QUARTER // TR
CHUNKS = [(p, t) for p in (0, 2, 1) for t in range(TILES)]
N = len(CHUNKS)
LENGTHS = (24, 26, 28, 31, 42)
REACH = 21
SPAN = WIDE + 2 * REACH

LANES = (slice(0, 128), slice(128, 256))
STEP_XY = 9.0 / 16
STEP_Z = 9.6 / TOTAL_VZ
CELL = STEP_XY * STEP_XY * STEP_Z


def kernel(
    cap,
    depth,
    sub,
    kick,
    rate,
    dens,
    kicked_out,
    coef,
    *scratch,
):
    scratch = list(scratch)
    take = lambda k: [scratch.pop(0) for _ in range(k)]
    block, packed, lists, chosen, moved = (take(N) for _ in range(5))
    planes, kick_wide, plane_sums, part, parts, kicked, order, local, remote_cols, mixed = take(10)
    y1_own, y1_out, y1_in, z_out, z_in, x_out, x_in = take(7)
    y2_own, y2_out, y2_in, halo_out, halo_in, sum_out, sum_in, kicked_sem = take(8)

    x, zh, y = (lax.axis_index(a) for a in GX)
    zl, core = (lax.axis_index(a) for a in VZ)
    nx = lax.axis_size("x")
    slab = zl * 2 + core
    slabs = lax.axis_size("zl") * 2

    def slab_device(v):
        return {"zl": v // 2, "core": v % 2}

    barrier = pltpu.get_barrier_semaphore()
    friends = [{"y": (y + k) % 4} for k in (1, 2, 3)]
    friends += [{"zh": 1 - zh}, {"x": (x + 1) % nx}, {"x": (x + nx - 1) % nx}]
    friends += [slab_device((slab + k) % slabs) for k in range(1, 8)]
    for friend in friends:
        pl.semaphore_signal(barrier, inc=1, device_id=friend, device_id_type=MESH)

    own = []
    for c, (p, t) in enumerate(CHUNKS):
        rows = pl.ds(y * QUARTER + t * TR, TR)
        own.append(pltpu.make_async_copy(dens.at[p, :, rows, :], block[c].at[pl.ds(y * COLS, COLS)], y1_own.at[c]))
        own[c].start()
    pl.semaphore_wait(barrier, len(friends))

    def remote(src, dst, send, recv, device):
        return pltpu.make_async_remote_copy(
            src_ref=src, dst_ref=dst, send_sem=send, recv_sem=recv, device_id=device, device_id_type=MESH
        )

    y1 = []
    for c, (p, t) in enumerate(CHUNKS):
        group = []
        for k in range(3):
            to = (y + k + 1) % 4
            rows = pl.ds(to * QUARTER + t * TR, TR)
            group.append(
                remote(
                    dens.at[p, :, rows, :],
                    block[c].at[pl.ds(y * COLS, COLS)],
                    y1_out.at[c, k],
                    y1_in.at[c, k],
                    {"y": to},
                )
            )
            group[-1].start()
        y1.append(group)

    depths = [depth[i] for i in range(NVX)]
    counts = [jnp.where(d >= 0, d + 1, -d) for d in depths]
    ranks = [jnp.int32(0)] * NVX
    for i in range(NVX):
        for j in range(i):
            behind = (counts[i] <= counts[j]).astype(jnp.int32)
            ranks[i] = ranks[i] + behind
            ranks[j] = ranks[j] + 1 - behind
    places = [jnp.where(r < 8, r, 23 - r) for r in ranks]

    def at_place(values, q):
        acc = values[0]
        for i in range(1, NVX):
            acc = jnp.where(places[i] == q, values[i], acc)
        return acc

    depths = [at_place(depths, q) for q in range(NVX)]
    far = [at_place([sub[i] for i in range(NVX)], q) for q in range(NVX)]
    counts = [jnp.where(d >= 0, d + 1, -d) for d in depths]
    edge = [REACH + jnp.where(d >= 0, WIDE - 1 - d, 0) for d in depths]
    upper = edge[:8]
    lower = [SPAN + edge[8 + s] - counts[s] for s in range(8)]
    lists_at = [jnp.where(d >= 0, 0, cap - d - REACH) for d in depths]
    for s in range(8):
        lists_at[8 + s] = lists_at[8 + s] + counts[s]

    to_lane = lax.broadcasted_iota(jnp.int32, (16, 256), 1)
    to_sub = lax.broadcasted_iota(jnp.int32, (16, 256), 0)
    for i in range(NVX):
        order[i * 16 : i * 16 + 16, :] = (to_lane == places[i] * 16 + to_sub).astype(jnp.bfloat16)

    def permute(values, back):
        total = None
        for _ in range(3):
            piece = values.astype(jnp.bfloat16)
            values = values - piece.astype(jnp.float32)
            term = lax.dot_general(
                piece, order[...], (((1,), (1 if back else 0,)), ((), ())), preferred_element_type=jnp.float32
            )
            total = term if total is None else total + term
        return total

    lane_group = lax.broadcasted_iota(jnp.int32, (TR, 128), 1) >> 4

    def by_group(values, h):
        acc = jnp.full((TR, 128), values[h * 8])
        for s in range(1, 8):
            acc = jnp.where(lane_group == s, values[h * 8 + s], acc)
        return acc

    lane_depth = [by_group(depths, h) for h in range(2)]
    lane_far = [by_group(far, h) for h in range(2)]

    pair = lax.broadcasted_iota(jnp.int32, (8, 256), 1)
    vx_of = ((pair >> 4).astype(jnp.float32) - 7.5) * STEP_XY
    vy_of = ((pair & 15).astype(jnp.float32) - 7.5) * STEP_XY
    which = lax.broadcasted_iota(jnp.int32, (8, 256), 0)
    weights = jnp.where(
        which == 0,
        1.0,
        jnp.where(which == 1, vx_of, jnp.where(which == 2, vy_of, jnp.where(which == 3, vx_of**2 + vy_of**2, 0.0))),
    )

    def spread(values, c):
        pick = (lax.broadcasted_iota(jnp.int32, (8, 128), 0) == c).astype(jnp.float32)
        return lax.dot_general(
            values, pick, (((0,), (0,)), ((), ())), precision=HIGH, preferred_element_type=jnp.float32
        )

    def widen_kick(c, _):
        kick_wide[c] = spread(kick[...], c)
        return 0

    lax.fori_loop(0, COLS, widen_kick, 0)

    @pl.when(slab == 0)
    def _():
        planes[0] = jnp.zeros((COLS, ROWS, 256), jnp.float32)

    @pl.when(slab == slabs - 1)
    def _():
        planes[4] = jnp.zeros((COLS, ROWS, 256), jnp.float32)

    z_copies, x_copies, y2, y2_self = {}, {}, {}, {}

    def stage_pack(c):
        own[c].wait()
        for copy in y1[c]:
            copy.wait_recv()

        for b in range(2):
            cols = slice(b * 16, b * 16 + 16)
            lined = permute(block[c][cols].reshape(16 * TR, 256), False)
            for h in range(2):
                at = h * SPAN + REACH + b * 16
                local[at : at + 16] = lined[:, LANES[h]].reshape(16, TR, 128)

        def one_row(r, _):
            acc = None
            for s in range(8):
                piece = local[r + jnp.where(r < counts[s], upper[s], lower[s])]
                acc = piece if s == 0 else jnp.where(lane_group == s, piece, acc)
            packed[c][r] = acc
            return 0

        lax.fori_loop(0, cap, one_row, 0)
        z_copies[c] = remote(
            packed[c], lists[c].at[pl.ds(zh * cap, cap)], z_out.at[c], z_in.at[c], {"zh": 1 - zh}
        )
        z_copies[c].start()

        def one_col(n, _):
            for h in range(2):
                acc = None
                for s in range(8):
                    piece = local[n + (h * SPAN + REACH - 1 - depths[h * 8 + s])]
                    acc = piece if s == 0 else jnp.where(lane_group == s, piece, acc)
                chosen[c][n, :, LANES[h]] = acc
            return 0

        lax.fori_loop(0, WIDE + 1, one_col, 0)

    def stage_forward(c):
        z_copies[c].wait_recv()
        x_copies[c] = remote(
            lists[c].at[pl.ds((1 - zh) * cap, cap)],
            lists[c].at[pl.ds(zh * cap, cap)],
            x_out.at[c],
            x_in.at[c],
            {"x": (x + 1 - 2 * zh + nx) % nx},
        )
        x_copies[c].start()

    def stage_merge(c):
        x_copies[c].wait_recv()
        p, t = CHUNKS[c]

        def one_remote(j, _):
            for h in range(2):
                acc = None
                for s in range(8):
                    piece = lists[c][j + lists_at[h * 8 + s]]
                    acc = piece if s == 0 else jnp.where(lane_group == s, piece, acc)
                remote_cols[j + 12, :, LANES[h]] = acc
            return 0

        lax.fori_loop(0, REACH, one_remote, 0)

        def column(n):
            got = []
            for h in range(2):
                from_col = n - 1 - lane_depth[h]
                inside = jnp.logical_and(from_col >= 0, from_col < WIDE)
                beyond = jnp.where(
                    lane_depth[h] >= 0, remote_cols[n + 12, :, LANES[h]], remote_cols[n, :, LANES[h]]
                )
                got.append(jnp.where(inside, chosen[c][n, :, LANES[h]], beyond))
            return got

        def one_col(n, before):
            now = column(n)
            for h in range(2):
                mixed[n - 1, :, LANES[h]] = (1.0 - lane_far[h]) * now[h] + lane_far[h] * before[h]
            return tuple(now)

        lax.fori_loop(1, WIDE + 1, one_col, tuple(column(0)))
        for b in range(2):
            cols = slice(b * 16, b * 16 + 16)
            moved[c][cols] = permute(mixed[cols].reshape(16 * TR, 256), True).reshape(16, TR, 256)
        here = planes.at[p + 1, :, pl.ds(y * QUARTER + t * TR, TR), :]
        y2[c] = []
        for k in range(3):
            to = (y + k + 1) % 4
            y2[c].append(
                remote(moved[c].at[pl.ds(to * COLS, COLS)], here, y2_out.at[c, k], y2_in.at[c, k], {"y": to})
            )
            y2[c][k].start()
        y2_self[c] = pltpu.make_async_copy(moved[c].at[pl.ds(y * COLS, COLS)], here, y2_own.at[c])
        y2_self[c].start()

    down = remote(planes.at[1], planes.at[4], halo_out.at[0], halo_in.at[0], slab_device((slab + slabs - 1) % slabs))
    up = remote(planes.at[3], planes.at[0], halo_out.at[1], halo_in.at[1], slab_device((slab + 1) % slabs))

    def stage_plane(p):
        for c, (q, _) in enumerate(CHUNKS):
            if q == p:
                y2_self[c].wait()
                for k in range(3):
                    y2[c][k].wait_recv()
        if p == 0:
            pl.when(slab > 0)(down.start)
        if p == 2:
            pl.when(slab < slabs - 1)(up.start)

        def one_col(c, _):
            plane_sums[p, c] = lax.dot_general(
                weights,
                planes[p + 1, c],
                (((1,), (1,)), ((), ())),
                precision=HIGH,
                preferred_element_type=jnp.float32,
            )
            return 0

        lax.fori_loop(0, COLS, one_col, 0)

    for name, c in ORDER:
        {"A": stage_pack, "B": stage_forward, "C": stage_merge, "D": stage_plane}[name](c)

    a = kick[...]
    lift, drop, stay = jnp.maximum(a, 0.0), jnp.maximum(-a, 0.0), 1.0 - jnp.abs(a)
    totals = [jnp.zeros((COLS, ROWS), jnp.float32) for _ in range(5)]
    for p in range(PLANES):
        level = slab * PLANES + p
        up_on = jnp.where(level + 1 < TOTAL_VZ, lift, 0.0)
        down_on = jnp.where(level >= 1, drop, 0.0)
        vz = (level.astype(jnp.float32) - 11.5) * STEP_Z
        above = ((level + 1).astype(jnp.float32) - 11.5) * STEP_Z
        below = ((level - 1).astype(jnp.float32) - 11.5) * STEP_Z
        kept = stay + up_on + down_on
        lean = stay * vz + up_on * above + down_on * below
        heat = stay * (vz * vz) + up_on * (above * above) + down_on * (below * below)
        n0, n1, n2, n3 = (plane_sums[p, :, j, :] for j in range(4))
        for j, term in enumerate((n0 * kept, n1 * kept, n2 * kept, n0 * lean, n3 * kept + n0 * heat)):
            totals[j] = totals[j] + term
    for j in range(5):
        part[j // 2, :, j % 2 * ROWS : (j % 2 + 1) * ROWS] = totals[j]

    shares = []
    for k in range(7):
        shares.append(remote(part, parts.at[k], sum_out.at[k], sum_in.at[k], slab_device((slab + k + 1) % slabs)))
        shares[k].start()
    pl.when(slab > 0)(up.wait_recv)
    pl.when(slab < slabs - 1)(down.wait_recv)

    def kick_col(c, _):
        a = kick_wide[c]
        lift, drop, stay = jnp.maximum(a, 0.0), jnp.maximum(-a, 0.0), 1.0 - jnp.abs(a)
        for lanes in LANES:
            for p in range(PLANES):
                kicked[p, c, :, lanes] = (
                    stay * planes[p + 1, c, :, lanes] + lift * planes[p, c, :, lanes] + drop * planes[p + 2, c, :, lanes]
                )
        return 0

    lax.fori_loop(0, COLS, kick_col, 0)
    kicked_copy = pltpu.make_async_copy(kicked, kicked_out, kicked_sem)
    kicked_copy.start()

    for k in range(7):
        shares[k].wait_recv()
    for j in range(5):
        for k in range(7):
            totals[j] = totals[j] + parts[k, j // 2, :, j % 2 * ROWS : (j % 2 + 1) * ROWS]

    mass = CELL * totals[0]
    flow_x = CELL * totals[1] / mass
    flow_y = CELL * totals[2] / mass
    flow_z = CELL * totals[3] / mass
    warm = (CELL * totals[4] - mass * (flow_x**2 + flow_y**2 + flow_z**2)) / (3.0 * mass)
    r = rate[...]
    share = 1.0 / (1.0 + r)
    two_pi_t = (2.0 * math.pi) * warm
    top = mass / (two_pi_t * jnp.sqrt(two_pi_t))
    for j, value in enumerate((share, r * share * top, -0.5 / warm, flow_x, flow_y, flow_z)):
        coef[j] = value

    kicked_copy.wait()
    pl.when(slab > 0)(down.wait_send)
    pl.when(slab < slabs - 1)(up.wait_send)
    for k in range(7):
        shares[k].wait_send()
    for c in range(N):
        z_copies[c].wait_send()
        x_copies[c].wait_send()
        for copy in y1[c] + y2[c]:
            copy.wait_send()


ORDER = tuple(zip("AAAAAABBCBCBCBDCBCDCD", (0, 1, 2, 3, 4, 5, 0, 1, 0, 2, 1, 3, 2, 4, 0, 3, 5, 4, 2, 5, 1)))


def step(cap, collective_id, density, shift_depth, sub_cell, gravity_kick, collision):
    f32 = jnp.float32
    vmem = pl.BlockSpec(memory_space=pltpu.VMEM)
    smem = pl.BlockSpec(memory_space=pltpu.SMEM)
    dma = pltpu.SemaphoreType.DMA
    return pl.pallas_call(
        functools.partial(kernel, cap),
        out_shape=(
            jax.ShapeDtypeStruct((PLANES, COLS, ROWS, 256), f32),
            jax.ShapeDtypeStruct((6, COLS, ROWS), f32),
        ),
        in_specs=[smem, smem, vmem, vmem, pl.BlockSpec(memory_space=pl.ANY)],
        out_specs=(pl.BlockSpec(memory_space=pl.ANY), vmem),
        scratch_shapes=[pltpu.VMEM((WIDE, TR, 256), f32)] * N
        + [pltpu.VMEM((cap, TR, 128), f32)] * N
        + [pltpu.VMEM((max(2 * cap, cap + 2 * REACH), TR, 128), f32)] * N
        + [pltpu.VMEM((WIDE + 1, TR, 256), f32)] * N
        + [pltpu.VMEM((WIDE, TR, 256), f32)] * N
        + [
            pltpu.VMEM((5, COLS, ROWS, 256), f32),
            pltpu.VMEM((COLS, ROWS, 128), f32),
            pltpu.VMEM((PLANES, COLS, 8, ROWS), f32),
            pltpu.VMEM((3, COLS, 128), f32),
            pltpu.VMEM((7, 3, COLS, 128), f32),
            pltpu.VMEM((PLANES, COLS, ROWS, 256), f32),
            pltpu.VMEM((256, 256), jnp.bfloat16),
            pltpu.VMEM((2 * SPAN + 2 * REACH, TR, 128), f32),
            pltpu.VMEM((REACH + 24, TR, 256), f32),
            pltpu.VMEM((WIDE, TR, 256), f32),
            dma((N,)),
            dma((N, 3)),
            dma((N, 3)),
            dma((N,)),
            dma((N,)),
            dma((N,)),
            dma((N,)),
            dma((N,)),
            dma((N, 3)),
            dma((N, 3)),
            dma((2,)),
            dma((2,)),
            dma((7,)),
            dma((7,)),
            dma,
        ],
        compiler_params=pltpu.CompilerParams(collective_id=collective_id, has_side_effects=True),
    )(shift_depth, sub_cell, gravity_kick, collision, density)


def rows_needed(shift_depth):
    count = jnp.where(shift_depth >= 0, shift_depth + 1, -shift_depth)
    place = jnp.arange(NVX, dtype=jnp.int32)
    ahead = (count[None, :] > count[:, None]) | ((count[None, :] == count[:, None]) & (place[None, :] < place[:, None]))
    rank = jnp.sum(ahead.astype(jnp.int32), axis=1)
    partner = rank[:, None] + rank[None, :] == NVX - 1
    return jnp.max(count + jnp.sum(jnp.where(partner, count[None, :], 0), axis=1))


def per_device(density, shift_depth, sub_cell, gravity_kick, collision):
    branches = [functools.partial(step, rows, k + 1) for k, rows in enumerate(LENGTHS)]
    branch = jnp.sum((rows_needed(shift_depth) > jnp.array(LENGTHS[:-1])).astype(jnp.int32))
    kicked, coef = lax.switch(branch, branches, density, shift_depth, sub_cell, gravity_kick, collision)
    keep, gain, cool, flow_x, flow_y, flow_z = (coef[j][:, :, None] for j in range(6))
    pair = jnp.arange(256, dtype=jnp.int32)
    vx = ((pair >> 4).astype(jnp.float32) - 7.5) * STEP_XY
    vy = ((pair & 15).astype(jnp.float32) - 7.5) * STEP_XY
    level = lax.axis_index(VZ) * PLANES + jnp.arange(PLANES, dtype=jnp.int32)
    vz = ((level.astype(jnp.float32) - 11.5) * STEP_Z)[:, None, None, None]
    flat = (vx - flow_x) ** 2 + (vy - flow_y) ** 2
    return keep * kicked + gain * jnp.exp(cool * (flat + (vz - flow_z) ** 2))


def solution(mesh):
    torus = Mesh(mesh.devices.reshape(mesh.shape["gx"] // 8, 2, 4, 4, 2), AXES)
    return jax.shard_map(
        per_device,
        mesh=torus,
        in_specs=(P(VZ, GX, None, None), P(), P(), P(GX, None), P(GX, None)),
        out_specs=P(VZ, GX, None, None),
        check_vma=False,
    )
```

```python
import functools
import math

import jax
import jax.numpy as jnp
from jax import lax
from jax.experimental import pallas as pl
from jax.experimental.pallas import tpu as pltpu
from jax.sharding import Mesh
from jax.sharding import PartitionSpec as P

AXES = ("x", "zh", "y", "zl", "core")
VZ = ("zl", "core")
GX = ("x", "zh", "y")
MESH = pl.DeviceIdType.MESH
HIGH = lax.Precision.HIGHEST

NVX = 16
COLS = 8
WIDE = 32
ROWS = 64
QUARTER = 16
PLANES = 3
TOTAL_VZ = 24
TR = 8
TILES = QUARTER // TR
CHUNKS = [(p, t) for p in (0, 2, 1) for t in range(TILES)]
N = len(CHUNKS)
LENGTHS = (24, 26, 28, 31, 42)
REACH = 21
SPAN = WIDE + 2 * REACH

LANES = (slice(0, 128), slice(128, 256))
STEP_XY = 9.0 / 16
STEP_Z = 9.6 / TOTAL_VZ
CELL = STEP_XY * STEP_XY * STEP_Z


def places_of(depth):
    depths = [depth[i] for i in range(NVX)]
    counts = [jnp.where(d >= 0, d + 1, -d) for d in depths]
    ranks = [jnp.int32(0)] * NVX
    for i in range(NVX):
        for j in range(i):
            behind = (counts[i] <= counts[j]).astype(jnp.int32)
            ranks[i] = ranks[i] + behind
            ranks[j] = ranks[j] + 1 - behind
    return depths, counts, [jnp.where(r < 8, r, 23 - r) for r in ranks]


def kernel(
    cap,
    depth,
    sub,
    kick,
    rate,
    dens,
    kicked_out,
    coef,
    *scratch,
):
    scratch = list(scratch)
    take = lambda k: [scratch.pop(0) for _ in range(k)]
    block, packed, lists, chosen, moved = (take(N) for _ in range(5))
    planes, kick_wide, plane_sums, part, parts, kicked, order, local, remote_cols, mixed = take(10)
    y1_own, y1_out, y1_in, z_out, z_in, x_out, x_in = take(7)
    y2_own, y2_out, y2_in, halo_out, halo_in, sum_out, sum_in, kicked_sem = take(8)

    x, zh, y = (lax.axis_index(a) for a in GX)
    zl, core = (lax.axis_index(a) for a in VZ)
    nx = lax.axis_size("x")
    slab = zl * 2 + core
    slabs = lax.axis_size("zl") * 2

    def slab_device(v):
        return {"zl": v // 2, "core": v % 2}

    barrier = pltpu.get_barrier_semaphore()
    friends = [{"y": (y + k) % 4} for k in (1, 2, 3)]
    friends += [{"zh": 1 - zh}, {"x": (x + 1) % nx}, {"x": (x + nx - 1) % nx}]
    friends += [slab_device((slab + k) % slabs) for k in range(1, 8)]
    for friend in friends:
        pl.semaphore_signal(barrier, inc=1, device_id=friend, device_id_type=MESH)

    own = []
    for c, (p, t) in enumerate(CHUNKS):
        rows = pl.ds(y * QUARTER + t * TR, TR)
        own.append(pltpu.make_async_copy(dens.at[p, :, rows, :], block[c].at[pl.ds(y * COLS, COLS)], y1_own.at[c]))
        own[c].start()
    pl.semaphore_wait(barrier, len(friends))

    def remote(src, dst, send, recv, device):
        return pltpu.make_async_remote_copy(
            src_ref=src, dst_ref=dst, send_sem=send, recv_sem=recv, device_id=device, device_id_type=MESH
        )

    y1 = []
    for c, (p, t) in enumerate(CHUNKS):
        group = []
        for k in range(3):
            to = (y + k + 1) % 4
            rows = pl.ds(to * QUARTER + t * TR, TR)
            group.append(
                remote(
                    dens.at[p, :, rows, :],
                    block[c].at[pl.ds(y * COLS, COLS)],
                    y1_out.at[c, k],
                    y1_in.at[c, k],
                    {"y": to},
                )
            )
            group[-1].start()
        y1.append(group)

    depths, counts, places = places_of(depth)

    def at_place(values, q):
        acc = values[0]
        for i in range(1, NVX):
            acc = jnp.where(places[i] == q, values[i], acc)
        return acc

    depths = [at_place(depths, q) for q in range(NVX)]
    far = [at_place([sub[i] for i in range(NVX)], q) for q in range(NVX)]
    counts = [jnp.where(d >= 0, d + 1, -d) for d in depths]
    edge = [REACH + jnp.where(d >= 0, WIDE - 1 - d, 0) for d in depths]
    upper = edge[:8]
    lower = [SPAN + edge[8 + s] - counts[s] for s in range(8)]
    lists_at = [jnp.where(d >= 0, 0, cap - d - REACH) for d in depths]
    for s in range(8):
        lists_at[8 + s] = lists_at[8 + s] + counts[s]

    to_lane = lax.broadcasted_iota(jnp.int32, (16, 256), 1)
    to_sub = lax.broadcasted_iota(jnp.int32, (16, 256), 0)
    for i in range(NVX):
        order[i * 16 : i * 16 + 16, :] = (to_lane == places[i] * 16 + to_sub).astype(jnp.bfloat16)

    def permute(values, back):
        total = None
        for _ in range(3):
            piece = values.astype(jnp.bfloat16)
            values = values - piece.astype(jnp.float32)
            term = lax.dot_general(
                piece, order[...], (((1,), (1 if back else 0,)), ((), ())), preferred_element_type=jnp.float32
            )
            total = term if total is None else total + term
        return total

    lane_group = lax.broadcasted_iota(jnp.int32, (TR, 128), 1) >> 4

    def by_group(values, h):
        acc = jnp.full((TR, 128), values[h * 8])
        for s in range(1, 8):
            acc = jnp.where(lane_group == s, values[h * 8 + s], acc)
        return acc

    lane_depth = [by_group(depths, h) for h in range(2)]
    lane_far = [by_group(far, h) for h in range(2)]

    pair = lax.broadcasted_iota(jnp.int32, (8, 256), 1)
    vx_odd = (pair >> 4) * 2 - 15
    vy_odd = (pair & 15) * 2 - 15
    which = lax.broadcasted_iota(jnp.int32, (8, 256), 0)
    weights = (
        jnp.where(
            which == 0,
            1,
            jnp.where(
                which == 1, vx_odd, jnp.where(which == 2, vy_odd, jnp.where(which == 3, (vx_odd**2 + vy_odd**2) >> 1, 0))
            ),
        )
        .astype(jnp.float32)
        .astype(jnp.bfloat16)
    )

    def spread(values, c):
        pick = (lax.broadcasted_iota(jnp.int32, (8, 128), 0) == c).astype(jnp.float32)
        return lax.dot_general(
            values, pick, (((0,), (0,)), ((), ())), precision=HIGH, preferred_element_type=jnp.float32
        )

    def widen_kick(c, _):
        kick_wide[c] = spread(kick[...], c)
        return 0

    lax.fori_loop(0, COLS, widen_kick, 0)

    @pl.when(slab == 0)
    def _():
        planes[0] = jnp.zeros((COLS, ROWS, 256), jnp.float32)

    @pl.when(slab == slabs - 1)
    def _():
        planes[4] = jnp.zeros((COLS, ROWS, 256), jnp.float32)

    z_copies, x_copies, y2, y2_self = {}, {}, {}, {}

    def stage_pack(c):
        own[c].wait()
        for copy in y1[c]:
            copy.wait_recv()

        for b in range(2):
            cols = slice(b * 16, b * 16 + 16)
            lined = permute(block[c][cols].reshape(16 * TR, 256), False)
            for h in range(2):
                at = h * SPAN + REACH + b * 16
                local[at : at + 16] = lined[:, LANES[h]].reshape(16, TR, 128)

        def one_row(r, _):
            acc = None
            for s in range(8):
                piece = local[r + jnp.where(r < counts[s], upper[s], lower[s])]
                acc = piece if s == 0 else jnp.where(lane_group == s, piece, acc)
            packed[c][r] = acc
            return 0

        lax.fori_loop(0, cap, one_row, 0)
        z_copies[c] = remote(
            packed[c], lists[c].at[pl.ds(zh * cap, cap)], z_out.at[c], z_in.at[c], {"zh": 1 - zh}
        )
        z_copies[c].start()

        def one_col(n, _):
            for h in range(2):
                acc = None
                for s in range(8):
                    piece = local[n + (h * SPAN + REACH - 1 - depths[h * 8 + s])]
                    acc = piece if s == 0 else jnp.where(lane_group == s, piece, acc)
                chosen[c][n, :, LANES[h]] = acc
            return 0

        lax.fori_loop(0, WIDE + 1, one_col, 0)

    def stage_forward(c):
        z_copies[c].wait_recv()
        x_copies[c] = remote(
            lists[c].at[pl.ds((1 - zh) * cap, cap)],
            lists[c].at[pl.ds(zh * cap, cap)],
            x_out.at[c],
            x_in.at[c],
            {"x": (x + 1 - 2 * zh + nx) % nx},
        )
        x_copies[c].start()

    def stage_merge(c):
        x_copies[c].wait_recv()
        p, t = CHUNKS[c]

        def one_remote(j, _):
            for h in range(2):
                acc = None
                for s in range(8):
                    piece = lists[c][j + lists_at[h * 8 + s]]
                    acc = piece if s == 0 else jnp.where(lane_group == s, piece, acc)
                remote_cols[j + 12, :, LANES[h]] = acc
            return 0

        lax.fori_loop(0, REACH, one_remote, 0)

        def column(n):
            got = []
            for h in range(2):
                from_col = n - 1 - lane_depth[h]
                inside = jnp.logical_and(from_col >= 0, from_col < WIDE)
                beyond = jnp.where(
                    lane_depth[h] >= 0, remote_cols[n + 12, :, LANES[h]], remote_cols[n, :, LANES[h]]
                )
                got.append(jnp.where(inside, chosen[c][n, :, LANES[h]], beyond))
            return got

        here = planes.at[p + 1, :, pl.ds(y * QUARTER + t * TR, TR), :]
        y2[c] = []
        for k in (1, 0, 2, 3):
            to = (y + k + 1) % 4

            def one_col(m, before):
                n = to * COLS + m
                now = column(n + 1)
                for h in range(2):
                    mixed[n, :, LANES[h]] = (1.0 - lane_far[h]) * now[h] + lane_far[h] * before[h]
                return tuple(now)

            lax.fori_loop(0, COLS, one_col, tuple(column(to * COLS)))
            cols = pl.ds(to * COLS, COLS)
            moved[c][cols] = permute(mixed[cols].reshape(COLS * TR, 256), True).reshape(COLS, TR, 256)
            if k < 3:
                y2[c].append(remote(moved[c].at[cols], here, y2_out.at[c, k], y2_in.at[c, k], {"y": to}))
                y2[c][-1].start()
        y2_self[c] = pltpu.make_async_copy(moved[c].at[pl.ds(y * COLS, COLS)], here, y2_own.at[c])
        y2_self[c].start()

    down = remote(planes.at[1], planes.at[4], halo_out.at[0], halo_in.at[0], slab_device((slab + slabs - 1) % slabs))
    up = remote(planes.at[3], planes.at[0], halo_out.at[1], halo_in.at[1], slab_device((slab + 1) % slabs))

    def stage_plane(p):
        for c, (q, _) in enumerate(CHUNKS):
            if q == p:
                y2_self[c].wait()
                for k in range(3):
                    y2[c][k].wait_recv()
        if p == 0:
            pl.when(slab > 0)(down.start)
        if p == 2:
            pl.when(slab < slabs - 1)(up.start)

        sums = None
        values = planes[p + 1].reshape(COLS * ROWS, 256)
        for _ in range(3):
            piece = values.astype(jnp.bfloat16)
            values = values - piece.astype(jnp.float32)
            term = lax.dot_general(weights, piece, (((1,), (1,)), ((), ())), preferred_element_type=jnp.float32)
            sums = term if sums is None else sums + term
        for c in range(COLS):
            plane_sums[p, c] = sums[:, c * ROWS : (c + 1) * ROWS]

    for name, c in ORDER:
        {"A": stage_pack, "B": stage_forward, "C": stage_merge, "D": stage_plane}[name](c)

    a = kick[...]
    lift, drop, stay = jnp.maximum(a, 0.0), jnp.maximum(-a, 0.0), 1.0 - jnp.abs(a)
    totals = [jnp.zeros((COLS, ROWS), jnp.float32) for _ in range(5)]
    for p in range(PLANES):
        level = slab * PLANES + p
        up_on = jnp.where(level + 1 < TOTAL_VZ, lift, 0.0)
        down_on = jnp.where(level >= 1, drop, 0.0)
        vz = (level.astype(jnp.float32) - 11.5) * STEP_Z
        above = ((level + 1).astype(jnp.float32) - 11.5) * STEP_Z
        below = ((level - 1).astype(jnp.float32) - 11.5) * STEP_Z
        kept = stay + up_on + down_on
        lean = stay * vz + up_on * above + down_on * below
        heat = stay * (vz * vz) + up_on * (above * above) + down_on * (below * below)
        n0, n1, n2, n3 = (
            unit * plane_sums[p, :, j, :] for j, unit in enumerate((1.0, STEP_XY / 2, STEP_XY / 2, STEP_XY**2 / 2))
        )
        for j, term in enumerate((n0 * kept, n1 * kept, n2 * kept, n0 * lean, n3 * kept + n0 * heat)):
            totals[j] = totals[j] + term
    for j in range(5):
        part[j // 2, :, j % 2 * ROWS : (j % 2 + 1) * ROWS] = totals[j]

    shares = []
    for k in range(7):
        shares.append(remote(part, parts.at[k], sum_out.at[k], sum_in.at[k], slab_device((slab + k + 1) % slabs)))
        shares[k].start()
    pl.when(slab > 0)(up.wait_recv)
    pl.when(slab < slabs - 1)(down.wait_recv)

    def kick_col(c, _):
        a = kick_wide[c]
        lift, drop, stay = jnp.maximum(a, 0.0), jnp.maximum(-a, 0.0), 1.0 - jnp.abs(a)
        for lanes in LANES:
            for p in range(PLANES):
                kicked[p, c, :, lanes] = (
                    stay * planes[p + 1, c, :, lanes] + lift * planes[p, c, :, lanes] + drop * planes[p + 2, c, :, lanes]
                )
        return 0

    lax.fori_loop(0, COLS, kick_col, 0)
    kicked_copy = pltpu.make_async_copy(kicked, kicked_out, kicked_sem)
    kicked_copy.start()

    for k in range(7):
        shares[k].wait_recv()
    for j in range(5):
        for k in range(7):
            totals[j] = totals[j] + parts[k, j // 2, :, j % 2 * ROWS : (j % 2 + 1) * ROWS]

    mass = CELL * totals[0]
    flow_x = CELL * totals[1] / mass
    flow_y = CELL * totals[2] / mass
    flow_z = CELL * totals[3] / mass
    warm = (CELL * totals[4] - mass * (flow_x**2 + flow_y**2 + flow_z**2)) / (3.0 * mass)
    r = rate[...]
    share = 1.0 / (1.0 + r)
    two_pi_t = (2.0 * math.pi) * warm
    top = mass / (two_pi_t * jnp.sqrt(two_pi_t))
    for j, value in enumerate((share, r * share * top, -0.5 / warm, flow_x, flow_y, flow_z)):
        coef[j] = value

    kicked_copy.wait()
    pl.when(slab > 0)(down.wait_send)
    pl.when(slab < slabs - 1)(up.wait_send)
    for k in range(7):
        shares[k].wait_send()
    for c in range(N):
        z_copies[c].wait_send()
        x_copies[c].wait_send()
        for copy in y1[c] + y2[c]:
            copy.wait_send()


ORDER = tuple(zip("AAAAAABBCBCBCBCBDCCDD", (0, 1, 2, 3, 4, 5, 0, 1, 0, 2, 1, 3, 2, 4, 3, 5, 0, 4, 5, 2, 1)))


def step(cap, collective_id, density, shift_depth, sub_cell, gravity_kick, collision):
    f32 = jnp.float32
    vmem = pl.BlockSpec(memory_space=pltpu.VMEM)
    smem = pl.BlockSpec(memory_space=pltpu.SMEM)
    dma = pltpu.SemaphoreType.DMA
    return pl.pallas_call(
        functools.partial(kernel, cap),
        out_shape=(
            jax.ShapeDtypeStruct((PLANES, COLS, ROWS, 256), f32),
            jax.ShapeDtypeStruct((6, COLS, ROWS), f32),
        ),
        in_specs=[smem, smem, vmem, vmem, pl.BlockSpec(memory_space=pl.ANY)],
        out_specs=(pl.BlockSpec(memory_space=pl.ANY), vmem),
        scratch_shapes=[pltpu.VMEM((WIDE, TR, 256), f32)] * N
        + [pltpu.VMEM((cap, TR, 128), f32)] * N
        + [pltpu.VMEM((max(2 * cap, cap + 2 * REACH), TR, 128), f32)] * N
        + [pltpu.VMEM((WIDE + 1, TR, 256), f32)] * N
        + [pltpu.VMEM((WIDE, TR, 256), f32)] * N
        + [
            pltpu.VMEM((5, COLS, ROWS, 256), f32),
            pltpu.VMEM((COLS, ROWS, 128), f32),
            pltpu.VMEM((PLANES, COLS, 8, ROWS), f32),
            pltpu.VMEM((3, COLS, 128), f32),
            pltpu.VMEM((7, 3, COLS, 128), f32),
            pltpu.VMEM((PLANES, COLS, ROWS, 256), f32),
            pltpu.VMEM((256, 256), jnp.bfloat16),
            pltpu.VMEM((2 * SPAN + 2 * REACH, TR, 128), f32),
            pltpu.VMEM((REACH + 24, TR, 256), f32),
            pltpu.VMEM((WIDE, TR, 256), f32),
            dma((N,)),
            dma((N, 3)),
            dma((N, 3)),
            dma((N,)),
            dma((N,)),
            dma((N,)),
            dma((N,)),
            dma((N,)),
            dma((N, 3)),
            dma((N, 3)),
            dma((2,)),
            dma((2,)),
            dma((7,)),
            dma((7,)),
            dma,
        ],
        compiler_params=pltpu.CompilerParams(collective_id=collective_id, has_side_effects=True),
    )(shift_depth, sub_cell, gravity_kick, collision, density)


def branch_kernel(depth, branch):
    _, counts, places = places_of(depth)
    need = jnp.int32(0)
    for i in range(NVX):
        for j in range(i):
            gap = places[i] - places[j]
            together = jnp.logical_or(gap == 8, gap == -8)
            need = jnp.maximum(need, jnp.where(together, counts[i] + counts[j], 0))
    k = jnp.int32(0)
    for rows in LENGTHS[:-1]:
        k = k + (need > rows).astype(jnp.int32)
    branch[0] = k


def per_device(density, shift_depth, sub_cell, gravity_kick, collision):
    branches = [functools.partial(step, rows, k + 1) for k, rows in enumerate(LENGTHS)]
    smem = pl.BlockSpec(memory_space=pltpu.SMEM)
    branch = pl.pallas_call(
        branch_kernel, out_shape=jax.ShapeDtypeStruct((1,), jnp.int32), in_specs=[smem], out_specs=smem
    )(shift_depth)[0]
    kicked, coef = lax.switch(branch, branches, density, shift_depth, sub_cell, gravity_kick, collision)
    keep, gain, cool, flow_x, flow_y, flow_z = (coef[j][:, :, None] for j in range(6))
    pair = jnp.arange(256, dtype=jnp.int32)
    vx = ((pair >> 4).astype(jnp.float32) - 7.5) * STEP_XY
    vy = ((pair & 15).astype(jnp.float32) - 7.5) * STEP_XY
    level = lax.axis_index(VZ) * PLANES + jnp.arange(PLANES, dtype=jnp.int32)
    vz = ((level.astype(jnp.float32) - 11.5) * STEP_Z)[:, None, None, None]
    flat = (vx - flow_x) ** 2 + (vy - flow_y) ** 2
    return keep * kicked + gain * jnp.exp(cool * (flat + (vz - flow_z) ** 2))


def solution(mesh):
    torus = Mesh(mesh.devices.reshape(mesh.shape["gx"] // 8, 2, 4, 4, 2), AXES)
    return jax.shard_map(
        per_device,
        mesh=torus,
        in_specs=(P(VZ, GX, None, None), P(), P(), P(GX, None), P(GX, None)),
        out_specs=P(VZ, GX, None, None),
        check_vma=False,
    )
```

```python
import functools
import math

import jax
import jax.numpy as jnp
from jax import lax
from jax.experimental import pallas as pl
from jax.experimental.pallas import tpu as pltpu
from jax.sharding import Mesh
from jax.sharding import PartitionSpec as P

AXES = ("x", "zh", "y", "zl", "core")
VZ = ("zl", "core")
GX = ("x", "zh", "y")
MESH = pl.DeviceIdType.MESH
HIGH = lax.Precision.HIGHEST

NVX = 16
COLS = 8
WIDE = 32
ROWS = 64
QUARTER = 16
PLANES = 3
TOTAL_VZ = 24
TR = 8
TILES = QUARTER // TR
CHUNKS = [(p, t) for p in (0, 2, 1) for t in range(TILES)]
N = len(CHUNKS)
LENGTHS = (23, 25, 26, 28, 30, 33, 42)
REACH = 21
SPAN = WIDE + 2 * REACH

LANES = (slice(0, 128), slice(128, 256))
STEP_XY = 9.0 / 16
STEP_Z = 9.6 / TOTAL_VZ
CELL = STEP_XY * STEP_XY * STEP_Z


def places_of(depth):
    depths = [depth[i] for i in range(NVX)]
    counts = [jnp.where(d >= 0, d + 1, -d) for d in depths]
    ranks = [jnp.int32(0)] * NVX
    for i in range(NVX):
        for j in range(i):
            behind = (counts[i] <= counts[j]).astype(jnp.int32)
            ranks[i] = ranks[i] + behind
            ranks[j] = ranks[j] + 1 - behind
    return depths, counts, [jnp.where(r < 8, r, 23 - r) for r in ranks]


def kernel(
    cap,
    depth,
    sub,
    kick,
    rate,
    dens,
    kicked_out,
    coef,
    *scratch,
):
    scratch = list(scratch)
    take = lambda k: [scratch.pop(0) for _ in range(k)]
    block, packed, lists, chosen, moved = (take(N) for _ in range(5))
    planes, kick_wide, plane_sums, part, parts, kicked, order, local, remote_cols, mixed = take(10)
    y1_own, y1_out, y1_in, z_out, z_in, x_out, x_in = take(7)
    y2_own, y2_out, y2_in, halo_out, halo_in, sum_out, sum_in, kicked_sem = take(8)

    x, zh, y = (lax.axis_index(a) for a in GX)
    zl, core = (lax.axis_index(a) for a in VZ)
    nx = lax.axis_size("x")
    slab = zl * 2 + core
    slabs = lax.axis_size("zl") * 2

    def slab_device(v):
        return {"zl": v // 2, "core": v % 2}

    barrier = pltpu.get_barrier_semaphore()
    friends = [{"y": (y + k) % 4} for k in (1, 2, 3)]
    friends += [{"zh": 1 - zh}, {"x": (x + 1) % nx}, {"x": (x + nx - 1) % nx}]
    friends += [slab_device((slab + k) % slabs) for k in range(1, 8)]
    for friend in friends:
        pl.semaphore_signal(barrier, inc=1, device_id=friend, device_id_type=MESH)

    own = []
    for c, (p, t) in enumerate(CHUNKS):
        rows = pl.ds(y * QUARTER + t * TR, TR)
        own.append(pltpu.make_async_copy(dens.at[p, :, rows, :], block[c].at[pl.ds(y * COLS, COLS)], y1_own.at[c]))
        own[c].start()
    pl.semaphore_wait(barrier, len(friends))

    def remote(src, dst, send, recv, device):
        return pltpu.make_async_remote_copy(
            src_ref=src, dst_ref=dst, send_sem=send, recv_sem=recv, device_id=device, device_id_type=MESH
        )

    for c, (p, t) in enumerate(CHUNKS):
        for k in range(3):
            to = (y + k + 1) % 4
            rows = pl.ds(to * QUARTER + t * TR, TR)
            remote(
                dens.at[p, :, rows, :], block[c].at[pl.ds(y * COLS, COLS)], y1_out.at[c], y1_in.at[c], {"y": to}
            ).start()

    def three(ref, send, recv):
        part = ref.at[pl.ds(0, 3 * COLS)]
        return remote(part, part, send, recv, {"y": (y + 1) % 4})

    y1 = [three(block[c], y1_out.at[c], y1_in.at[c]) for c in range(N)]
    y2 = [three(moved[c], y2_out.at[c], y2_in.at[c]) for c in range(N)]

    depths, counts, places = places_of(depth)

    def at_place(values, q):
        acc = values[0]
        for i in range(1, NVX):
            acc = jnp.where(places[i] == q, values[i], acc)
        return acc

    depths = [at_place(depths, q) for q in range(NVX)]
    far = [at_place([sub[i] for i in range(NVX)], q) for q in range(NVX)]
    counts = [jnp.where(d >= 0, d + 1, -d) for d in depths]
    edge = [REACH + jnp.where(d >= 0, WIDE - 1 - d, 0) for d in depths]
    upper = edge[:8]
    lower = [SPAN + edge[8 + s] - counts[s] for s in range(8)]
    lists_at = [jnp.where(d >= 0, 0, cap - d - REACH) for d in depths]
    for s in range(8):
        lists_at[8 + s] = lists_at[8 + s] + counts[s]

    to_lane = lax.broadcasted_iota(jnp.int32, (16, 256), 1)
    to_sub = lax.broadcasted_iota(jnp.int32, (16, 256), 0)
    for i in range(NVX):
        order[i * 16 : i * 16 + 16, :] = (to_lane == places[i] * 16 + to_sub).astype(jnp.bfloat16)

    def permute(values, back):
        total = None
        for _ in range(3):
            piece = values.astype(jnp.bfloat16)
            values = values - piece.astype(jnp.float32)
            term = lax.dot_general(
                piece, order[...], (((1,), (1 if back else 0,)), ((), ())), preferred_element_type=jnp.float32
            )
            total = term if total is None else total + term
        return total

    lane_group = lax.broadcasted_iota(jnp.int32, (TR, 128), 1) >> 4

    def by_group(values, h):
        acc = jnp.full((TR, 128), values[h * 8])
        for s in range(1, 8):
            acc = jnp.where(lane_group == s, values[h * 8 + s], acc)
        return acc

    lane_depth = [by_group(depths, h) for h in range(2)]
    lane_far = [by_group(far, h) for h in range(2)]

    pair = lax.broadcasted_iota(jnp.int32, (8, 256), 1)
    vx_odd = (pair >> 4) * 2 - 15
    vy_odd = (pair & 15) * 2 - 15
    which = lax.broadcasted_iota(jnp.int32, (8, 256), 0)
    weights = (
        jnp.where(
            which == 0,
            1,
            jnp.where(
                which == 1, vx_odd, jnp.where(which == 2, vy_odd, jnp.where(which == 3, (vx_odd**2 + vy_odd**2) >> 1, 0))
            ),
        )
        .astype(jnp.float32)
        .astype(jnp.bfloat16)
    )

    def spread(values, c):
        pick = (lax.broadcasted_iota(jnp.int32, (8, 128), 0) == c).astype(jnp.float32)
        return lax.dot_general(
            values, pick, (((0,), (0,)), ((), ())), precision=HIGH, preferred_element_type=jnp.float32
        )

    def widen_kick(c, _):
        kick_wide[c] = spread(kick[...], c)
        return 0

    lax.fori_loop(0, COLS, widen_kick, 0)

    @pl.when(slab == 0)
    def _():
        planes[0] = jnp.zeros((COLS, ROWS, 256), jnp.float32)

    @pl.when(slab == slabs - 1)
    def _():
        planes[4] = jnp.zeros((COLS, ROWS, 256), jnp.float32)

    z_copies, x_copies, y2_self = {}, {}, {}
    pieces = [(c, 0, cap) for c in range(N - 1)] + [(N - 1, 0, cap // 2), (N - 1, cap // 2, cap)]

    def stage_pack(c):
        own[c].wait()
        y1[c].wait_recv()

        def line_up(b, _):
            cols = pl.ds(b * COLS, COLS)
            lined = permute(block[c][cols].reshape(COLS * TR, 256), False)
            for h in range(2):
                local[pl.ds(h * SPAN + REACH + b * COLS, COLS)] = lined[:, LANES[h]].reshape(COLS, TR, 128)
            return 0

        lax.fori_loop(0, 4, line_up, 0)

        def one_row(r, _):
            acc = None
            for s in range(8):
                piece = local[r + jnp.where(r < counts[s], upper[s], lower[s])]
                acc = piece if s == 0 else jnp.where(lane_group == s, piece, acc)
            packed[c][r] = acc
            return 0

        lax.fori_loop(0, cap, one_row, 0)
        for e, (q, low, high) in enumerate(pieces):
            if q == c:
                z_copies[e] = remote(
                    packed[c].at[pl.ds(low, high - low)],
                    lists[c].at[pl.ds(zh * cap + low, high - low)],
                    z_out.at[e],
                    z_in.at[e],
                    {"zh": 1 - zh},
                )
                z_copies[e].start()

        def one_col(n, _):
            for h in range(2):
                acc = None
                for s in range(8):
                    piece = local[n + (h * SPAN + REACH - 1 - depths[h * 8 + s])]
                    acc = piece if s == 0 else jnp.where(lane_group == s, piece, acc)
                chosen[c][n, :, LANES[h]] = acc
            return 0

        lax.fori_loop(0, WIDE + 1, one_col, 0)

    def stage_forward(e):
        c, low, high = pieces[e]
        z_copies[e].wait_recv()
        x_copies[e] = remote(
            lists[c].at[pl.ds((1 - zh) * cap + low, high - low)],
            lists[c].at[pl.ds(zh * cap + low, high - low)],
            x_out.at[e],
            x_in.at[e],
            {"x": (x + 1 - 2 * zh + nx) % nx},
        )
        x_copies[e].start()

    def stage_merge(c):
        for e, (q, _, _) in enumerate(pieces):
            if q == c:
                x_copies[e].wait_recv()
        p, t = CHUNKS[c]

        def one_remote(j, _):
            for h in range(2):
                acc = None
                for s in range(8):
                    piece = lists[c][j + lists_at[h * 8 + s]]
                    acc = piece if s == 0 else jnp.where(lane_group == s, piece, acc)
                remote_cols[j + 12, :, LANES[h]] = acc
            return 0

        lax.fori_loop(0, REACH, one_remote, 0)

        def column(n):
            got = []
            for h in range(2):
                from_col = n - 1 - lane_depth[h]
                inside = jnp.logical_and(from_col >= 0, from_col < WIDE)
                beyond = jnp.where(
                    lane_depth[h] >= 0, remote_cols[n + 12, :, LANES[h]], remote_cols[n, :, LANES[h]]
                )
                got.append(jnp.where(inside, chosen[c][n, :, LANES[h]], beyond))
            return got

        here = planes.at[p + 1, :, pl.ds(y * QUARTER + t * TR, TR), :]
        y2_self[c] = pltpu.make_async_copy(moved[c].at[pl.ds(y * COLS, COLS)], here, y2_own.at[c])

        def one_target(k, _):
            to = (y + k + 1) % 4

            def one_col(m, before):
                n = to * COLS + m
                now = column(n + 1)
                for h in range(2):
                    mixed[n, :, LANES[h]] = (1.0 - lane_far[h]) * now[h] + lane_far[h] * before[h]
                return tuple(now)

            lax.fori_loop(0, COLS, one_col, tuple(column(to * COLS)))
            cols = pl.ds(to * COLS, COLS)
            moved[c][cols] = permute(mixed[cols].reshape(COLS * TR, 256), True).reshape(COLS, TR, 256)

            @pl.when(k < 3)
            def _():
                remote(moved[c].at[cols], here, y2_out.at[c], y2_in.at[c], {"y": to}).start()

            return 0

        lax.fori_loop(0, 4, one_target, 0)
        y2_self[c].start()

    down = remote(planes.at[1], planes.at[4], halo_out.at[0], halo_in.at[0], slab_device((slab + slabs - 1) % slabs))
    up = remote(planes.at[3], planes.at[0], halo_out.at[1], halo_in.at[1], slab_device((slab + 1) % slabs))

    def stage_plane(p):
        for c, (q, _) in enumerate(CHUNKS):
            if q == p:
                y2_self[c].wait()
                y2[c].wait_recv()
        if p == 0:
            pl.when(slab > 0)(down.start)
        if p == 2:
            pl.when(slab < slabs - 1)(up.start)

        def four_cols(b, _):
            sums = None
            values = planes[p + 1, pl.ds(b * 4, 4)].reshape(4 * ROWS, 256)
            for _ in range(3):
                piece = values.astype(jnp.bfloat16)
                values = values - piece.astype(jnp.float32)
                term = lax.dot_general(weights, piece, (((1,), (1,)), ((), ())), preferred_element_type=jnp.float32)
                sums = term if sums is None else sums + term
            for c in range(4):
                plane_sums[p, b * 4 + c] = sums[:, c * ROWS : (c + 1) * ROWS]
            return 0

        for b in range(2):
            four_cols(b, 0)

    for name, c in ORDER:
        {"A": stage_pack, "B": stage_forward, "C": stage_merge, "D": stage_plane}[name](c)

    a = kick[...]
    lift, drop, stay = jnp.maximum(a, 0.0), jnp.maximum(-a, 0.0), 1.0 - jnp.abs(a)
    totals = [jnp.zeros((COLS, ROWS), jnp.float32) for _ in range(5)]
    for p in range(PLANES):
        level = slab * PLANES + p
        up_on = jnp.where(level + 1 < TOTAL_VZ, lift, 0.0)
        down_on = jnp.where(level >= 1, drop, 0.0)
        vz = (level.astype(jnp.float32) - 11.5) * STEP_Z
        above = ((level + 1).astype(jnp.float32) - 11.5) * STEP_Z
        below = ((level - 1).astype(jnp.float32) - 11.5) * STEP_Z
        kept = stay + up_on + down_on
        lean = stay * vz + up_on * above + down_on * below
        heat = stay * (vz * vz) + up_on * (above * above) + down_on * (below * below)
        n0, n1, n2, n3 = (
            unit * plane_sums[p, :, j, :] for j, unit in enumerate((1.0, STEP_XY / 2, STEP_XY / 2, STEP_XY**2 / 2))
        )
        for j, term in enumerate((n0 * kept, n1 * kept, n2 * kept, n0 * lean, n3 * kept + n0 * heat)):
            totals[j] = totals[j] + term
    for j in range(5):
        part[j // 2, :, j % 2 * ROWS : (j % 2 + 1) * ROWS] = totals[j]

    for k in range(7):
        remote(part, parts.at[k], sum_out, sum_in, slab_device((slab + k + 1) % slabs)).start()
    shares = remote(parts, parts, sum_out, sum_in, slab_device((slab + 1) % slabs))
    pl.when(slab > 0)(up.wait_recv)
    pl.when(slab < slabs - 1)(down.wait_recv)

    def kick_col(c, _):
        a = kick_wide[c]
        lift, drop, stay = jnp.maximum(a, 0.0), jnp.maximum(-a, 0.0), 1.0 - jnp.abs(a)
        for lanes in LANES:
            for p in range(PLANES):
                kicked[p, c, :, lanes] = (
                    stay * planes[p + 1, c, :, lanes] + lift * planes[p, c, :, lanes] + drop * planes[p + 2, c, :, lanes]
                )
        return 0

    lax.fori_loop(0, COLS, kick_col, 0)
    kicked_copy = pltpu.make_async_copy(kicked, kicked_out, kicked_sem)
    kicked_copy.start()

    shares.wait_recv()
    for j in range(5):
        for k in range(7):
            totals[j] = totals[j] + parts[k, j // 2, :, j % 2 * ROWS : (j % 2 + 1) * ROWS]

    mass = CELL * totals[0]
    flow_x = CELL * totals[1] / mass
    flow_y = CELL * totals[2] / mass
    flow_z = CELL * totals[3] / mass
    warm = (CELL * totals[4] - mass * (flow_x**2 + flow_y**2 + flow_z**2)) / (3.0 * mass)
    r = rate[...]
    share = 1.0 / (1.0 + r)
    two_pi_t = (2.0 * math.pi) * warm
    top = mass / (two_pi_t * jnp.sqrt(two_pi_t))
    for j, value in enumerate((share, r * share * top, -0.5 / warm, flow_x, flow_y, flow_z)):
        coef[j] = value

    kicked_copy.wait()
    pl.when(slab > 0)(down.wait_send)
    pl.when(slab < slabs - 1)(up.wait_send)
    shares.wait_send()
    for e in range(len(pieces)):
        z_copies[e].wait_send()
        x_copies[e].wait_send()
    for c in range(N):
        y1[c].wait_send()
        y2[c].wait_send()


ORDER = tuple(zip("AAAAAABBCBCBCBCBDBCCDD", (0, 1, 2, 3, 4, 5, 0, 1, 0, 2, 1, 3, 2, 4, 3, 5, 0, 6, 4, 5, 2, 1)))


def step(cap, collective_id, density, shift_depth, sub_cell, gravity_kick, collision):
    f32 = jnp.float32
    vmem = pl.BlockSpec(memory_space=pltpu.VMEM)
    smem = pl.BlockSpec(memory_space=pltpu.SMEM)
    dma = pltpu.SemaphoreType.DMA
    return pl.pallas_call(
        functools.partial(kernel, cap),
        out_shape=(
            jax.ShapeDtypeStruct((PLANES, COLS, ROWS, 256), f32),
            jax.ShapeDtypeStruct((6, COLS, ROWS), f32),
        ),
        in_specs=[smem, smem, vmem, vmem, pl.BlockSpec(memory_space=pl.ANY)],
        out_specs=(pl.BlockSpec(memory_space=pl.ANY), vmem),
        scratch_shapes=[pltpu.VMEM((WIDE, TR, 256), f32)] * N
        + [pltpu.VMEM((cap, TR, 128), f32)] * N
        + [pltpu.VMEM((max(2 * cap, cap + 2 * REACH), TR, 128), f32)] * N
        + [pltpu.VMEM((WIDE + 1, TR, 256), f32)] * N
        + [pltpu.VMEM((WIDE, TR, 256), f32)] * N
        + [
            pltpu.VMEM((5, COLS, ROWS, 256), f32),
            pltpu.VMEM((COLS, ROWS, 128), f32),
            pltpu.VMEM((PLANES, COLS, 8, ROWS), f32),
            pltpu.VMEM((3, COLS, 128), f32),
            pltpu.VMEM((7, 3, COLS, 128), f32),
            pltpu.VMEM((PLANES, COLS, ROWS, 256), f32),
            pltpu.VMEM((256, 256), jnp.bfloat16),
            pltpu.VMEM((2 * SPAN + 2 * REACH, TR, 128), f32),
            pltpu.VMEM((REACH + 24, TR, 256), f32),
            pltpu.VMEM((WIDE, TR, 256), f32),
            dma((N,)),
            dma((N,)),
            dma((N,)),
            dma((N + 1,)),
            dma((N + 1,)),
            dma((N + 1,)),
            dma((N + 1,)),
            dma((N,)),
            dma((N,)),
            dma((N,)),
            dma((2,)),
            dma((2,)),
            dma,
            dma,
            dma,
        ],
        compiler_params=pltpu.CompilerParams(collective_id=collective_id, has_side_effects=True),
    )(shift_depth, sub_cell, gravity_kick, collision, density)


def branch_kernel(depth, branch):
    _, counts, places = places_of(depth)
    need = jnp.int32(0)
    for i in range(NVX):
        for j in range(i):
            gap = places[i] - places[j]
            together = jnp.logical_or(gap == 8, gap == -8)
            need = jnp.maximum(need, jnp.where(together, counts[i] + counts[j], 0))
    k = jnp.int32(0)
    for rows in LENGTHS[:-1]:
        k = k + (need > rows).astype(jnp.int32)
    branch[0] = k


def per_device(density, shift_depth, sub_cell, gravity_kick, collision):
    branches = [functools.partial(step, rows, k + 1) for k, rows in enumerate(LENGTHS)]
    smem = pl.BlockSpec(memory_space=pltpu.SMEM)
    branch = pl.pallas_call(
        branch_kernel, out_shape=jax.ShapeDtypeStruct((1,), jnp.int32), in_specs=[smem], out_specs=smem
    )(shift_depth)[0]
    kicked, coef = lax.switch(branch, branches, density, shift_depth, sub_cell, gravity_kick, collision)
    keep, gain, cool, flow_x, flow_y, flow_z = (coef[j][:, :, None] for j in range(6))
    pair = jnp.arange(256, dtype=jnp.int32)
    vx = ((pair >> 4).astype(jnp.float32) - 7.5) * STEP_XY
    vy = ((pair & 15).astype(jnp.float32) - 7.5) * STEP_XY
    level = lax.axis_index(VZ) * PLANES + jnp.arange(PLANES, dtype=jnp.int32)
    vz = ((level.astype(jnp.float32) - 11.5) * STEP_Z)[:, None, None, None]
    flat = (vx - flow_x) ** 2 + (vy - flow_y) ** 2
    return keep * kicked + gain * jnp.exp(cool * (flat + (vz - flow_z) ** 2))


def solution(mesh):
    torus = Mesh(mesh.devices.reshape(mesh.shape["gx"] // 8, 2, 4, 4, 2), AXES)
    return jax.shard_map(
        per_device,
        mesh=torus,
        in_specs=(P(VZ, GX, None, None), P(), P(), P(GX, None), P(GX, None)),
        out_specs=P(VZ, GX, None, None),
        check_vma=False,
    )
```

```python
import functools
import math

import jax
import jax.numpy as jnp
from jax import lax
from jax.experimental import pallas as pl
from jax.experimental.pallas import tpu as pltpu
from jax.sharding import Mesh
from jax.sharding import PartitionSpec as P

AXES = ("x", "zh", "y", "zl", "core")
VZ = ("zl", "core")
GX = ("x", "zh", "y")
MESH = pl.DeviceIdType.MESH
HIGH = lax.Precision.HIGHEST

NVX = 16
COLS = 8
WIDE = 32
ROWS = 64
QUARTER = 16
PLANES = 3
TOTAL_VZ = 24
TR = 8
TILES = QUARTER // TR
CHUNKS = [(p, t) for p in (0, 2, 1) for t in range(TILES)]
N = len(CHUNKS)
LENGTHS = (23, 25, 26, 28, 30, 33, 42)
REACH = 21
SPAN = WIDE + 2 * REACH

LANES = (slice(0, 128), slice(128, 256))
STEP_XY = 9.0 / 16
STEP_Z = 9.6 / TOTAL_VZ
CELL = STEP_XY * STEP_XY * STEP_Z


def places_of(depth):
    depths = [depth[i] for i in range(NVX)]
    counts = [jnp.where(d >= 0, d + 1, -d) for d in depths]
    ranks = [jnp.int32(0)] * NVX
    for i in range(NVX):
        for j in range(i):
            behind = (counts[i] <= counts[j]).astype(jnp.int32)
            ranks[i] = ranks[i] + behind
            ranks[j] = ranks[j] + 1 - behind
    return depths, counts, [jnp.where(r < 8, r, 23 - r) for r in ranks]


def kernel(
    cap,
    depth,
    sub,
    kick,
    rate,
    dens,
    kicked_out,
    coef,
    *scratch,
):
    scratch = list(scratch)
    take = lambda k: [scratch.pop(0) for _ in range(k)]
    block, packed, lists, chosen, moved = (take(N) for _ in range(5))
    planes, kick_wide, plane_sums, part, parts, kicked, order, local, remote_cols, mixed = take(10)
    y1_own, y1_out, y1_in, z_out, z_in, x_out, x_in = take(7)
    y2_own, y2_out, y2_in, halo_out, halo_in, sum_out, sum_in, kicked_sem = take(8)

    x, zh, y = (lax.axis_index(a) for a in GX)
    zl, core = (lax.axis_index(a) for a in VZ)
    nx = lax.axis_size("x")
    slab = zl * 2 + core
    slabs = lax.axis_size("zl") * 2

    def slab_device(v):
        return {"zl": v // 2, "core": v % 2}

    barrier = pltpu.get_barrier_semaphore()
    friends = [{"y": (y + k) % 4} for k in (1, 2, 3)]
    friends += [{"zh": 1 - zh}, {"x": (x + 1) % nx}, {"x": (x + nx - 1) % nx}]
    friends += [slab_device((slab + k) % slabs) for k in range(1, 8)]
    for friend in friends:
        pl.semaphore_signal(barrier, inc=1, device_id=friend, device_id_type=MESH)

    own = []
    for c, (p, t) in enumerate(CHUNKS):
        rows = pl.ds(y * QUARTER + t * TR, TR)
        own.append(pltpu.make_async_copy(dens.at[p, :, rows, :], block[c].at[pl.ds(y * COLS, COLS)], y1_own.at[c]))
        own[c].start()
    pl.semaphore_wait(barrier, len(friends))

    def remote(src, dst, send, recv, device):
        return pltpu.make_async_remote_copy(
            src_ref=src, dst_ref=dst, send_sem=send, recv_sem=recv, device_id=device, device_id_type=MESH
        )

    for c, (p, t) in enumerate(CHUNKS):
        for k in range(3):
            to = (y + k + 1) % 4
            rows = pl.ds(to * QUARTER + t * TR, TR)
            remote(
                dens.at[p, :, rows, :], block[c].at[pl.ds(y * COLS, COLS)], y1_out.at[c], y1_in.at[c], {"y": to}
            ).start()

    def three(ref, send, recv):
        part = ref.at[pl.ds(0, 3 * COLS)]
        return remote(part, part, send, recv, {"y": (y + 1) % 4})

    y1 = [three(block[c], y1_out.at[c], y1_in.at[c]) for c in range(N)]
    y2 = [three(moved[c], y2_out.at[c], y2_in.at[c]) for c in range(N)]

    depths, counts, places = places_of(depth)

    def at_place(values, q):
        acc = values[0]
        for i in range(1, NVX):
            acc = jnp.where(places[i] == q, values[i], acc)
        return acc

    depths = [at_place(depths, q) for q in range(NVX)]
    far = [at_place([sub[i] for i in range(NVX)], q) for q in range(NVX)]
    counts = [jnp.where(d >= 0, d + 1, -d) for d in depths]
    edge = [REACH + jnp.where(d >= 0, WIDE - 1 - d, 0) for d in depths]
    upper = edge[:8]
    lower = [SPAN + edge[8 + s] - counts[s] for s in range(8)]
    lists_at = [jnp.where(d >= 0, 0, cap - d - REACH) for d in depths]
    for s in range(8):
        lists_at[8 + s] = lists_at[8 + s] + counts[s]

    to_lane = lax.broadcasted_iota(jnp.int32, (16, 256), 1)
    to_sub = lax.broadcasted_iota(jnp.int32, (16, 256), 0)
    for i in range(NVX):
        order[i * 16 : i * 16 + 16, :] = (to_lane == places[i] * 16 + to_sub).astype(jnp.bfloat16)

    def permute(values, back):
        total = None
        for _ in range(3):
            piece = values.astype(jnp.bfloat16)
            values = values - piece.astype(jnp.float32)
            term = lax.dot_general(
                piece, order[...], (((1,), (1 if back else 0,)), ((), ())), preferred_element_type=jnp.float32
            )
            total = term if total is None else total + term
        return total

    lane_group = lax.broadcasted_iota(jnp.int32, (TR, 128), 1) >> 4

    def by_group(values, h):
        acc = jnp.full((TR, 128), values[h * 8])
        for s in range(1, 8):
            acc = jnp.where(lane_group == s, values[h * 8 + s], acc)
        return acc

    lane_depth = [by_group(depths, h) for h in range(2)]
    lane_far = [by_group(far, h) for h in range(2)]

    pair = lax.broadcasted_iota(jnp.int32, (8, 256), 1)
    vx_odd = (pair >> 4) * 2 - 15
    vy_odd = (pair & 15) * 2 - 15
    which = lax.broadcasted_iota(jnp.int32, (8, 256), 0)
    weights = (
        jnp.where(
            which == 0,
            1,
            jnp.where(
                which == 1, vx_odd, jnp.where(which == 2, vy_odd, jnp.where(which == 3, (vx_odd**2 + vy_odd**2) >> 1, 0))
            ),
        )
        .astype(jnp.float32)
        .astype(jnp.bfloat16)
    )

    def spread(values, c):
        pick = (lax.broadcasted_iota(jnp.int32, (8, 128), 0) == c).astype(jnp.float32)
        return lax.dot_general(
            values, pick, (((0,), (0,)), ((), ())), precision=HIGH, preferred_element_type=jnp.float32
        )

    def widen_kick(c, _):
        kick_wide[c] = spread(kick[...], c)
        return 0

    lax.fori_loop(0, COLS, widen_kick, 0)

    @pl.when(slab == 0)
    def _():
        planes[0] = jnp.zeros((COLS, ROWS, 256), jnp.float32)

    @pl.when(slab == slabs - 1)
    def _():
        planes[4] = jnp.zeros((COLS, ROWS, 256), jnp.float32)

    z_copies, x_copies, y2_self = {}, {}, {}
    pieces = [(c, 0, cap) for c in range(N - 1)] + [(N - 1, 0, cap // 2), (N - 1, cap // 2, cap)]

    def stage_pack(c):
        own[c].wait()
        y1[c].wait_recv()

        def line_up(b, _):
            cols = pl.ds(b * COLS, COLS)
            lined = permute(block[c][cols].reshape(COLS * TR, 256), False)
            for h in range(2):
                local[pl.ds(h * SPAN + REACH + b * COLS, COLS)] = lined[:, LANES[h]].reshape(COLS, TR, 128)
            return 0

        if c == 0:
            for b in range(4):
                line_up(b, 0)
        else:
            lax.fori_loop(0, 4, line_up, 0)

        def one_row(r, _):
            acc = None
            for s in range(8):
                piece = local[r + jnp.where(r < counts[s], upper[s], lower[s])]
                acc = piece if s == 0 else jnp.where(lane_group == s, piece, acc)
            packed[c][r] = acc
            return 0

        lax.fori_loop(0, cap, one_row, 0)
        for e, (q, low, high) in enumerate(pieces):
            if q == c:
                z_copies[e] = remote(
                    packed[c].at[pl.ds(low, high - low)],
                    lists[c].at[pl.ds(zh * cap + low, high - low)],
                    z_out.at[e],
                    z_in.at[e],
                    {"zh": 1 - zh},
                )
                z_copies[e].start()

        def one_col(n, _):
            for h in range(2):
                acc = None
                for s in range(8):
                    piece = local[n + (h * SPAN + REACH - 1 - depths[h * 8 + s])]
                    acc = piece if s == 0 else jnp.where(lane_group == s, piece, acc)
                chosen[c][n, :, LANES[h]] = acc
            return 0

        lax.fori_loop(0, WIDE + 1, one_col, 0)

    def stage_forward(e):
        c, low, high = pieces[e]
        z_copies[e].wait_recv()
        x_copies[e] = remote(
            lists[c].at[pl.ds((1 - zh) * cap + low, high - low)],
            lists[c].at[pl.ds(zh * cap + low, high - low)],
            x_out.at[e],
            x_in.at[e],
            {"x": (x + 1 - 2 * zh + nx) % nx},
        )
        x_copies[e].start()

    def stage_merge(c):
        for e, (q, _, _) in enumerate(pieces):
            if q == c:
                x_copies[e].wait_recv()
        p, t = CHUNKS[c]

        def one_remote(j, _):
            for h in range(2):
                acc = None
                for s in range(8):
                    piece = lists[c][j + lists_at[h * 8 + s]]
                    acc = piece if s == 0 else jnp.where(lane_group == s, piece, acc)
                remote_cols[j + 12, :, LANES[h]] = acc
            return 0

        lax.fori_loop(0, REACH, one_remote, 0)

        def column(n):
            got = []
            for h in range(2):
                from_col = n - 1 - lane_depth[h]
                inside = jnp.logical_and(from_col >= 0, from_col < WIDE)
                beyond = jnp.where(
                    lane_depth[h] >= 0, remote_cols[n + 12, :, LANES[h]], remote_cols[n, :, LANES[h]]
                )
                got.append(jnp.where(inside, chosen[c][n, :, LANES[h]], beyond))
            return got

        here = planes.at[p + 1, :, pl.ds(y * QUARTER + t * TR, TR), :]
        y2_self[c] = pltpu.make_async_copy(moved[c].at[pl.ds(y * COLS, COLS)], here, y2_own.at[c])

        def one_target(k, _):
            to = (y + k + 1) % 4

            def one_col(m, before):
                n = to * COLS + m
                now = column(n + 1)
                for h in range(2):
                    mixed[n, :, LANES[h]] = (1.0 - lane_far[h]) * now[h] + lane_far[h] * before[h]
                return tuple(now)

            lax.fori_loop(0, COLS, one_col, tuple(column(to * COLS)))
            cols = pl.ds(to * COLS, COLS)
            moved[c][cols] = permute(mixed[cols].reshape(COLS * TR, 256), True).reshape(COLS, TR, 256)

            @pl.when(k < 3)
            def _():
                remote(moved[c].at[cols], here, y2_out.at[c], y2_in.at[c], {"y": to}).start()

            return 0

        lax.fori_loop(0, 4, one_target, 0)
        y2_self[c].start()

    down = remote(planes.at[1], planes.at[4], halo_out.at[0], halo_in.at[0], slab_device((slab + slabs - 1) % slabs))
    up = remote(planes.at[3], planes.at[0], halo_out.at[1], halo_in.at[1], slab_device((slab + 1) % slabs))

    def stage_plane(p):
        for c, (q, _) in enumerate(CHUNKS):
            if q == p:
                y2_self[c].wait()
                y2[c].wait_recv()
        if p == 0:
            pl.when(slab > 0)(down.start)
        if p == 2:
            pl.when(slab < slabs - 1)(up.start)

        def four_cols(b, _):
            sums = None
            values = planes[p + 1, pl.ds(b * 4, 4)].reshape(4 * ROWS, 256)
            for _ in range(3):
                piece = values.astype(jnp.bfloat16)
                values = values - piece.astype(jnp.float32)
                term = lax.dot_general(weights, piece, (((1,), (1,)), ((), ())), preferred_element_type=jnp.float32)
                sums = term if sums is None else sums + term
            for c in range(4):
                plane_sums[p, b * 4 + c] = sums[:, c * ROWS : (c + 1) * ROWS]
            return 0

        for b in range(2):
            four_cols(b, 0)

    for name, c in ORDER:
        {"A": stage_pack, "B": stage_forward, "C": stage_merge, "D": stage_plane}[name](c)

    a = kick[...]
    lift, drop, stay = jnp.maximum(a, 0.0), jnp.maximum(-a, 0.0), 1.0 - jnp.abs(a)
    totals = [jnp.zeros((COLS, ROWS), jnp.float32) for _ in range(5)]
    for p in range(PLANES):
        level = slab * PLANES + p
        up_on = jnp.where(level + 1 < TOTAL_VZ, lift, 0.0)
        down_on = jnp.where(level >= 1, drop, 0.0)
        vz = (level.astype(jnp.float32) - 11.5) * STEP_Z
        above = ((level + 1).astype(jnp.float32) - 11.5) * STEP_Z
        below = ((level - 1).astype(jnp.float32) - 11.5) * STEP_Z
        kept = stay + up_on + down_on
        lean = stay * vz + up_on * above + down_on * below
        heat = stay * (vz * vz) + up_on * (above * above) + down_on * (below * below)
        n0, n1, n2, n3 = (
            unit * plane_sums[p, :, j, :] for j, unit in enumerate((1.0, STEP_XY / 2, STEP_XY / 2, STEP_XY**2 / 2))
        )
        for j, term in enumerate((n0 * kept, n1 * kept, n2 * kept, n0 * lean, n3 * kept + n0 * heat)):
            totals[j] = totals[j] + term
    for j in range(5):
        part[j // 2, :, j % 2 * ROWS : (j % 2 + 1) * ROWS] = totals[j]

    for k in range(7):
        remote(part, parts.at[k], sum_out, sum_in, slab_device((slab + k + 1) % slabs)).start()
    shares = remote(parts, parts, sum_out, sum_in, slab_device((slab + 1) % slabs))
    pl.when(slab > 0)(up.wait_recv)
    pl.when(slab < slabs - 1)(down.wait_recv)

    def kick_col(c, _):
        a = kick_wide[c]
        lift, drop, stay = jnp.maximum(a, 0.0), jnp.maximum(-a, 0.0), 1.0 - jnp.abs(a)
        for lanes in LANES:
            for p in range(PLANES):
                kicked[p, c, :, lanes] = (
                    stay * planes[p + 1, c, :, lanes] + lift * planes[p, c, :, lanes] + drop * planes[p + 2, c, :, lanes]
                )
        return 0

    lax.fori_loop(0, COLS, kick_col, 0)
    kicked_copy = pltpu.make_async_copy(kicked, kicked_out, kicked_sem)
    kicked_copy.start()

    shares.wait_recv()
    for j in range(5):
        for k in range(7):
            totals[j] = totals[j] + parts[k, j // 2, :, j % 2 * ROWS : (j % 2 + 1) * ROWS]

    mass = CELL * totals[0]
    flow_x = CELL * totals[1] / mass
    flow_y = CELL * totals[2] / mass
    flow_z = CELL * totals[3] / mass
    warm = (CELL * totals[4] - mass * (flow_x**2 + flow_y**2 + flow_z**2)) / (3.0 * mass)
    r = rate[...]
    share = 1.0 / (1.0 + r)
    two_pi_t = (2.0 * math.pi) * warm
    top = mass / (two_pi_t * jnp.sqrt(two_pi_t))
    for j, value in enumerate((share, r * share * top, -0.5 / warm, flow_x, flow_y, flow_z)):
        coef[j] = value

    kicked_copy.wait()
    pl.when(slab > 0)(down.wait_send)
    pl.when(slab < slabs - 1)(up.wait_send)
    shares.wait_send()
    for e in range(len(pieces)):
        z_copies[e].wait_send()
        x_copies[e].wait_send()
    for c in range(N):
        y1[c].wait_send()
        y2[c].wait_send()


ORDER = tuple(zip("AAAAAABBCBCBCBCBDBCCDD", (0, 1, 2, 3, 4, 5, 0, 1, 0, 2, 1, 3, 2, 4, 3, 5, 0, 6, 4, 5, 2, 1)))


def step(cap, collective_id, density, shift_depth, sub_cell, gravity_kick, collision):
    f32 = jnp.float32
    vmem = pl.BlockSpec(memory_space=pltpu.VMEM)
    smem = pl.BlockSpec(memory_space=pltpu.SMEM)
    dma = pltpu.SemaphoreType.DMA
    return pl.pallas_call(
        functools.partial(kernel, cap),
        out_shape=(
            jax.ShapeDtypeStruct((PLANES, COLS, ROWS, 256), f32),
            jax.ShapeDtypeStruct((6, COLS, ROWS), f32),
        ),
        in_specs=[smem, smem, vmem, vmem, pl.BlockSpec(memory_space=pl.ANY)],
        out_specs=(pl.BlockSpec(memory_space=pl.ANY), vmem),
        scratch_shapes=[pltpu.VMEM((WIDE, TR, 256), f32)] * N
        + [pltpu.VMEM((cap, TR, 128), f32)] * N
        + [pltpu.VMEM((max(2 * cap, cap + 2 * REACH), TR, 128), f32)] * N
        + [pltpu.VMEM((WIDE + 1, TR, 256), f32)] * N
        + [pltpu.VMEM((WIDE, TR, 256), f32)] * N
        + [
            pltpu.VMEM((5, COLS, ROWS, 256), f32),
            pltpu.VMEM((COLS, ROWS, 128), f32),
            pltpu.VMEM((PLANES, COLS, 8, ROWS), f32),
            pltpu.VMEM((3, COLS, 128), f32),
            pltpu.VMEM((7, 3, COLS, 128), f32),
            pltpu.VMEM((PLANES, COLS, ROWS, 256), f32),
            pltpu.VMEM((256, 256), jnp.bfloat16),
            pltpu.VMEM((2 * SPAN + 2 * REACH, TR, 128), f32),
            pltpu.VMEM((REACH + 24, TR, 256), f32),
            pltpu.VMEM((WIDE, TR, 256), f32),
            dma((N,)),
            dma((N,)),
            dma((N,)),
            dma((N + 1,)),
            dma((N + 1,)),
            dma((N + 1,)),
            dma((N + 1,)),
            dma((N,)),
            dma((N,)),
            dma((N,)),
            dma((2,)),
            dma((2,)),
            dma,
            dma,
            dma,
        ],
        compiler_params=pltpu.CompilerParams(collective_id=collective_id, has_side_effects=True),
    )(shift_depth, sub_cell, gravity_kick, collision, density)


def branch_kernel(depth, branch):
    _, counts, places = places_of(depth)
    need = jnp.int32(0)
    for i in range(NVX):
        for j in range(i):
            gap = places[i] - places[j]
            together = jnp.logical_or(gap == 8, gap == -8)
            need = jnp.maximum(need, jnp.where(together, counts[i] + counts[j], 0))
    k = jnp.int32(0)
    for rows in LENGTHS[:-1]:
        k = k + (need > rows).astype(jnp.int32)
    branch[0] = k


def per_device(density, shift_depth, sub_cell, gravity_kick, collision):
    branches = [functools.partial(step, rows, k + 1) for k, rows in enumerate(LENGTHS)]
    smem = pl.BlockSpec(memory_space=pltpu.SMEM)
    branch = pl.pallas_call(
        branch_kernel, out_shape=jax.ShapeDtypeStruct((1,), jnp.int32), in_specs=[smem], out_specs=smem
    )(shift_depth)[0]
    kicked, coef = lax.switch(branch, branches, density, shift_depth, sub_cell, gravity_kick, collision)
    keep, gain, cool, flow_x, flow_y, flow_z = (coef[j][:, :, None] for j in range(6))
    pair = jnp.arange(256, dtype=jnp.int32)
    vx = ((pair >> 4).astype(jnp.float32) - 7.5) * STEP_XY
    vy = ((pair & 15).astype(jnp.float32) - 7.5) * STEP_XY
    level = lax.axis_index(VZ) * PLANES + jnp.arange(PLANES, dtype=jnp.int32)
    vz = ((level.astype(jnp.float32) - 11.5) * STEP_Z)[:, None, None, None]
    flat = (vx - flow_x) ** 2 + (vy - flow_y) ** 2
    return keep * kicked + gain * jnp.exp(cool * (flat + (vz - flow_z) ** 2))


def solution(mesh):
    torus = Mesh(mesh.devices.reshape(mesh.shape["gx"] // 8, 2, 4, 4, 2), AXES)
    return jax.shard_map(
        per_device,
        mesh=torus,
        in_specs=(P(VZ, GX, None, None), P(), P(), P(GX, None), P(GX, None)),
        out_specs=P(VZ, GX, None, None),
        check_vma=False,
    )
```

```python
import functools
import math

import jax
import jax.numpy as jnp
from jax import lax
from jax.experimental import pallas as pl
from jax.experimental.pallas import tpu as pltpu
from jax.sharding import Mesh
from jax.sharding import PartitionSpec as P

AXES = ("x", "zh", "y", "zl", "core")
VZ = ("zl", "core")
GX = ("x", "zh", "y")
MESH = pl.DeviceIdType.MESH
HIGH = lax.Precision.HIGHEST

NVX = 16
COLS = 8
WIDE = 32
ROWS = 64
QUARTER = 16
PLANES = 3
TOTAL_VZ = 24
TR = 8
TILES = QUARTER // TR
CHUNKS = [(p, t) for p in (0, 2, 1) for t in range(TILES)]
N = len(CHUNKS)
LENGTHS = (23, 25, 27, 29, 31, 34, 42)
REACH = 21
SPAN = WIDE + 2 * REACH

LANES = (slice(0, 128), slice(128, 256))
STEP_XY = 9.0 / 16
STEP_Z = 9.6 / TOTAL_VZ
CELL = STEP_XY * STEP_XY * STEP_Z


def places_of(depth):
    depths = [depth[i] for i in range(NVX)]
    counts = [jnp.where(d >= 0, d + 1, -d) for d in depths]
    ranks = [jnp.int32(0)] * NVX
    for i in range(NVX):
        for j in range(i):
            behind = (counts[i] <= counts[j]).astype(jnp.int32)
            ranks[i] = ranks[i] + behind
            ranks[j] = ranks[j] + 1 - behind
    return depths, counts, [jnp.where(r < 8, r, 23 - r) for r in ranks]


def kernel(
    cap,
    depth,
    sub,
    kick,
    rate,
    dens,
    kicked_out,
    coef,
    *scratch,
):
    scratch = list(scratch)
    take = lambda k: [scratch.pop(0) for _ in range(k)]
    block, packed, lists, chosen, moved = (take(N) for _ in range(5))
    planes, kick_wide, plane_sums, part, parts, kicked, order, local, remote_cols, mixed = take(10)
    y1_own, y1_out, y1_in, z_out, z_in, x_out, x_in = take(7)
    y2_own, y2_out, y2_in, halo_out, halo_in, sum_out, sum_in, kicked_sem = take(8)

    x, zh, y = (lax.axis_index(a) for a in GX)
    zl, core = (lax.axis_index(a) for a in VZ)
    nx = lax.axis_size("x")
    slab = zl * 2 + core
    slabs = lax.axis_size("zl") * 2

    def slab_device(v):
        return {"zl": v // 2, "core": v % 2}

    barrier = pltpu.get_barrier_semaphore()
    friends = [{"y": (y + k) % 4} for k in (1, 2, 3)]
    friends += [{"zh": 1 - zh}, {"x": (x + 1) % nx}, {"x": (x + nx - 1) % nx}]
    friends += [slab_device((slab + k) % slabs) for k in range(1, 8)]
    for friend in friends:
        pl.semaphore_signal(barrier, inc=1, device_id=friend, device_id_type=MESH)

    own = []
    for c, (p, t) in enumerate(CHUNKS):
        rows = pl.ds(y * QUARTER + t * TR, TR)
        own.append(pltpu.make_async_copy(dens.at[p, :, rows, :], block[c].at[pl.ds(y * COLS, COLS)], y1_own.at[c]))
        own[c].start()
    pl.semaphore_wait(barrier, len(friends))

    def remote(src, dst, send, recv, device):
        return pltpu.make_async_remote_copy(
            src_ref=src, dst_ref=dst, send_sem=send, recv_sem=recv, device_id=device, device_id_type=MESH
        )

    for c, (p, t) in enumerate(CHUNKS):
        for k in range(3):
            to = (y + k + 1) % 4
            rows = pl.ds(to * QUARTER + t * TR, TR)
            remote(
                dens.at[p, :, rows, :], block[c].at[pl.ds(y * COLS, COLS)], y1_out.at[c], y1_in.at[c], {"y": to}
            ).start()

    def three(ref, send, recv):
        part = ref.at[pl.ds(0, 3 * COLS)]
        return remote(part, part, send, recv, {"y": (y + 1) % 4})

    y1 = [three(block[c], y1_out.at[c], y1_in.at[c]) for c in range(N)]
    y2 = [three(moved[c], y2_out.at[c], y2_in.at[c]) for c in range(N)]

    depths, counts, places = places_of(depth)

    def at_place(values, q):
        acc = values[0]
        for i in range(1, NVX):
            acc = jnp.where(places[i] == q, values[i], acc)
        return acc

    depths = [at_place(depths, q) for q in range(NVX)]
    far = [at_place([sub[i] for i in range(NVX)], q) for q in range(NVX)]
    counts = [jnp.where(d >= 0, d + 1, -d) for d in depths]
    edge = [REACH + jnp.where(d >= 0, WIDE - 1 - d, 0) for d in depths]
    upper = edge[:8]
    lower = [SPAN + edge[8 + s] - counts[s] for s in range(8)]
    lists_at = [jnp.where(d >= 0, 0, cap - d - REACH) for d in depths]
    for s in range(8):
        lists_at[8 + s] = lists_at[8 + s] + counts[s]

    to_lane = lax.broadcasted_iota(jnp.int32, (16, 256), 1)
    to_sub = lax.broadcasted_iota(jnp.int32, (16, 256), 0)
    for i in range(NVX):
        order[i * 16 : i * 16 + 16, :] = (to_lane == places[i] * 16 + to_sub).astype(jnp.bfloat16)

    def permute(values, back):
        total = None
        for _ in range(3):
            piece = values.astype(jnp.bfloat16)
            values = values - piece.astype(jnp.float32)
            term = lax.dot_general(
                piece, order[...], (((1,), (1 if back else 0,)), ((), ())), preferred_element_type=jnp.float32
            )
            total = term if total is None else total + term
        return total

    lane_group = lax.broadcasted_iota(jnp.int32, (TR, 128), 1) >> 4

    def by_group(values, h):
        acc = jnp.full((TR, 128), values[h * 8])
        for s in range(1, 8):
            acc = jnp.where(lane_group == s, values[h * 8 + s], acc)
        return acc

    lane_depth = [by_group(depths, h) for h in range(2)]
    lane_far = [by_group(far, h) for h in range(2)]

    pair = lax.broadcasted_iota(jnp.int32, (8, 256), 1)
    vx_odd = (pair >> 4) * 2 - 15
    vy_odd = (pair & 15) * 2 - 15
    which = lax.broadcasted_iota(jnp.int32, (8, 256), 0)
    weights = (
        jnp.where(
            which == 0,
            1,
            jnp.where(
                which == 1, vx_odd, jnp.where(which == 2, vy_odd, jnp.where(which == 3, (vx_odd**2 + vy_odd**2) >> 1, 0))
            ),
        )
        .astype(jnp.float32)
        .astype(jnp.bfloat16)
    )

    def spread(values, c):
        pick = (lax.broadcasted_iota(jnp.int32, (8, 128), 0) == c).astype(jnp.float32)
        return lax.dot_general(
            values, pick, (((0,), (0,)), ((), ())), precision=HIGH, preferred_element_type=jnp.float32
        )

    def widen_kick(c, _):
        kick_wide[c] = spread(kick[...], c)
        return 0

    lax.fori_loop(0, COLS, widen_kick, 0)

    @pl.when(slab == 0)
    def _():
        planes[0] = jnp.zeros((COLS, ROWS, 256), jnp.float32)

    @pl.when(slab == slabs - 1)
    def _():
        planes[4] = jnp.zeros((COLS, ROWS, 256), jnp.float32)

    z_copies, x_copies, y2_self = {}, {}, {}
    pieces = [(c, 0, cap) for c in range(N - 1)] + [(N - 1, 0, cap // 2), (N - 1, cap // 2, cap)]

    def stage_pack(c):
        own[c].wait()
        y1[c].wait_recv()

        def line_up(b, _):
            cols = pl.ds(b * COLS, COLS)
            lined = permute(block[c][cols].reshape(COLS * TR, 256), False)
            for h in range(2):
                local[pl.ds(h * SPAN + REACH + b * COLS, COLS)] = lined[:, LANES[h]].reshape(COLS, TR, 128)
            return 0

        if c == 0:
            for b in range(4):
                line_up(b, 0)
        else:
            lax.fori_loop(0, 4, line_up, 0)

        def one_row(r, _):
            acc = None
            for s in range(8):
                piece = local[r + jnp.where(r < counts[s], upper[s], lower[s])]
                acc = piece if s == 0 else jnp.where(lane_group == s, piece, acc)
            packed[c][r] = acc
            return 0

        lax.fori_loop(0, cap, one_row, 0)
        for e, (q, low, high) in enumerate(pieces):
            if q == c:
                z_copies[e] = remote(
                    packed[c].at[pl.ds(low, high - low)],
                    lists[c].at[pl.ds(zh * cap + low, high - low)],
                    z_out.at[e],
                    z_in.at[e],
                    {"zh": 1 - zh},
                )
                z_copies[e].start()

        def one_col(n, _):
            for h in range(2):
                acc = None
                for s in range(8):
                    piece = local[n + (h * SPAN + REACH - 1 - depths[h * 8 + s])]
                    acc = piece if s == 0 else jnp.where(lane_group == s, piece, acc)
                chosen[c][n, :, LANES[h]] = acc
            return 0

        lax.fori_loop(0, WIDE + 1, one_col, 0)

    def stage_forward(e):
        c, low, high = pieces[e]
        z_copies[e].wait_recv()
        x_copies[e] = remote(
            lists[c].at[pl.ds((1 - zh) * cap + low, high - low)],
            lists[c].at[pl.ds(zh * cap + low, high - low)],
            x_out.at[e],
            x_in.at[e],
            {"x": (x + 1 - 2 * zh + nx) % nx},
        )
        x_copies[e].start()

    def stage_merge(c):
        for e, (q, _, _) in enumerate(pieces):
            if q == c:
                x_copies[e].wait_recv()
        p, t = CHUNKS[c]

        def one_remote(j, _):
            for h in range(2):
                acc = None
                for s in range(8):
                    piece = lists[c][j + lists_at[h * 8 + s]]
                    acc = piece if s == 0 else jnp.where(lane_group == s, piece, acc)
                remote_cols[j + 12, :, LANES[h]] = acc
            return 0

        lax.fori_loop(0, REACH, one_remote, 0)

        def column(n):
            got = []
            for h in range(2):
                from_col = n - 1 - lane_depth[h]
                inside = jnp.logical_and(from_col >= 0, from_col < WIDE)
                beyond = jnp.where(
                    lane_depth[h] >= 0, remote_cols[n + 12, :, LANES[h]], remote_cols[n, :, LANES[h]]
                )
                got.append(jnp.where(inside, chosen[c][n, :, LANES[h]], beyond))
            return got

        here = planes.at[p + 1, :, pl.ds(y * QUARTER + t * TR, TR), :]
        y2_self[c] = pltpu.make_async_copy(moved[c].at[pl.ds(y * COLS, COLS)], here, y2_own.at[c])

        def one_target(k, _):
            to = (y + k + 1) % 4

            def one_col(m, before):
                n = to * COLS + m
                now = column(n + 1)
                for h in range(2):
                    mixed[n, :, LANES[h]] = (1.0 - lane_far[h]) * now[h] + lane_far[h] * before[h]
                return tuple(now)

            lax.fori_loop(0, COLS, one_col, tuple(column(to * COLS)))
            cols = pl.ds(to * COLS, COLS)
            moved[c][cols] = permute(mixed[cols].reshape(COLS * TR, 256), True).reshape(COLS, TR, 256)

            @pl.when(k < 3)
            def _():
                remote(moved[c].at[cols], here, y2_out.at[c], y2_in.at[c], {"y": to}).start()

            return 0

        lax.fori_loop(0, 4, one_target, 0)
        y2_self[c].start()

    down = remote(planes.at[1], planes.at[4], halo_out.at[0], halo_in.at[0], slab_device((slab + slabs - 1) % slabs))
    up = remote(planes.at[3], planes.at[0], halo_out.at[1], halo_in.at[1], slab_device((slab + 1) % slabs))

    a = kick[...]
    lift, drop, stay = jnp.maximum(a, 0.0), jnp.maximum(-a, 0.0), 1.0 - jnp.abs(a)
    totals = [jnp.zeros((COLS, ROWS), jnp.float32) for _ in range(5)]

    def stage_plane(p):
        for c, (q, _) in enumerate(CHUNKS):
            if q == p:
                y2_self[c].wait()
                y2[c].wait_recv()
        if p == 0:
            pl.when(slab > 0)(down.start)
        if p == 2:
            pl.when(slab < slabs - 1)(up.start)

        def four_cols(b, _):
            sums = None
            values = planes[p + 1, pl.ds(b * 4, 4)].reshape(4 * ROWS, 256)
            for _ in range(3):
                piece = values.astype(jnp.bfloat16)
                values = values - piece.astype(jnp.float32)
                term = lax.dot_general(weights, piece, (((1,), (1,)), ((), ())), preferred_element_type=jnp.float32)
                sums = term if sums is None else sums + term
            for c in range(4):
                plane_sums[p, b * 4 + c] = sums[:, c * ROWS : (c + 1) * ROWS]
            return 0

        for b in range(2):
            four_cols(b, 0)

        level = slab * PLANES + p
        up_on = jnp.where(level + 1 < TOTAL_VZ, lift, 0.0)
        down_on = jnp.where(level >= 1, drop, 0.0)
        vz = (level.astype(jnp.float32) - 11.5) * STEP_Z
        above = ((level + 1).astype(jnp.float32) - 11.5) * STEP_Z
        below = ((level - 1).astype(jnp.float32) - 11.5) * STEP_Z
        kept = stay + up_on + down_on
        lean = stay * vz + up_on * above + down_on * below
        heat = stay * (vz * vz) + up_on * (above * above) + down_on * (below * below)
        n0, n1, n2, n3 = (
            unit * plane_sums[p, :, j, :] for j, unit in enumerate((1.0, STEP_XY / 2, STEP_XY / 2, STEP_XY**2 / 2))
        )
        for j, term in enumerate((n0 * kept, n1 * kept, n2 * kept, n0 * lean, n3 * kept + n0 * heat)):
            totals[j] = totals[j] + term

    for name, c in ORDER:
        {"A": stage_pack, "B": stage_forward, "C": stage_merge, "D": stage_plane}[name](c)

    for j in range(5):
        part[j // 2, :, j % 2 * ROWS : (j % 2 + 1) * ROWS] = totals[j]

    for k in range(7):
        remote(part, parts.at[k], sum_out, sum_in, slab_device((slab + k + 1) % slabs)).start()
    shares = remote(parts, parts, sum_out, sum_in, slab_device((slab + 1) % slabs))
    pl.when(slab > 0)(up.wait_recv)
    pl.when(slab < slabs - 1)(down.wait_recv)

    def kick_col(c, _):
        a = kick_wide[c]
        lift, drop, stay = jnp.maximum(a, 0.0), jnp.maximum(-a, 0.0), 1.0 - jnp.abs(a)
        for lanes in LANES:
            for p in range(PLANES):
                kicked[p, c, :, lanes] = (
                    stay * planes[p + 1, c, :, lanes] + lift * planes[p, c, :, lanes] + drop * planes[p + 2, c, :, lanes]
                )
        return 0

    lax.fori_loop(0, COLS, kick_col, 0)
    kicked_copy = pltpu.make_async_copy(kicked, kicked_out, kicked_sem)
    kicked_copy.start()

    shares.wait_recv()
    for j in range(5):
        for k in range(7):
            totals[j] = totals[j] + parts[k, j // 2, :, j % 2 * ROWS : (j % 2 + 1) * ROWS]

    mass = CELL * totals[0]
    flow_x = CELL * totals[1] / mass
    flow_y = CELL * totals[2] / mass
    flow_z = CELL * totals[3] / mass
    warm = (CELL * totals[4] - mass * (flow_x**2 + flow_y**2 + flow_z**2)) / (3.0 * mass)
    r = rate[...]
    share = 1.0 / (1.0 + r)
    two_pi_t = (2.0 * math.pi) * warm
    top = mass / (two_pi_t * jnp.sqrt(two_pi_t))
    for j, value in enumerate((share, r * share * top, -0.5 / warm, flow_x, flow_y, flow_z)):
        coef[j] = value

    kicked_copy.wait()
    pl.when(slab > 0)(down.wait_send)
    pl.when(slab < slabs - 1)(up.wait_send)
    shares.wait_send()
    for e in range(len(pieces)):
        z_copies[e].wait_send()
        x_copies[e].wait_send()
    for c in range(N):
        y1[c].wait_send()
        y2[c].wait_send()


ORDER = tuple(zip("AAAAAABBCBCBCBCBDBCCDD", (0, 1, 2, 3, 4, 5, 0, 1, 0, 2, 1, 3, 2, 4, 3, 5, 0, 6, 4, 5, 2, 1)))


def step(cap, collective_id, density, shift_depth, sub_cell, gravity_kick, collision):
    f32 = jnp.float32
    vmem = pl.BlockSpec(memory_space=pltpu.VMEM)
    smem = pl.BlockSpec(memory_space=pltpu.SMEM)
    dma = pltpu.SemaphoreType.DMA
    return pl.pallas_call(
        functools.partial(kernel, cap),
        out_shape=(
            jax.ShapeDtypeStruct((PLANES, COLS, ROWS, 256), f32),
            jax.ShapeDtypeStruct((6, COLS, ROWS), f32),
        ),
        in_specs=[smem, smem, vmem, vmem, pl.BlockSpec(memory_space=pl.ANY)],
        out_specs=(pl.BlockSpec(memory_space=pl.ANY), vmem),
        scratch_shapes=[pltpu.VMEM((WIDE, TR, 256), f32)] * N
        + [pltpu.VMEM((cap, TR, 128), f32)] * N
        + [pltpu.VMEM((max(2 * cap, cap + 2 * REACH), TR, 128), f32)] * N
        + [pltpu.VMEM((WIDE + 1, TR, 256), f32)] * N
        + [pltpu.VMEM((WIDE, TR, 256), f32)] * N
        + [
            pltpu.VMEM((5, COLS, ROWS, 256), f32),
            pltpu.VMEM((COLS, ROWS, 128), f32),
            pltpu.VMEM((PLANES, COLS, 8, ROWS), f32),
            pltpu.VMEM((3, COLS, 128), f32),
            pltpu.VMEM((7, 3, COLS, 128), f32),
            pltpu.VMEM((PLANES, COLS, ROWS, 256), f32),
            pltpu.VMEM((256, 256), jnp.bfloat16),
            pltpu.VMEM((2 * SPAN + 2 * REACH, TR, 128), f32),
            pltpu.VMEM((REACH + 24, TR, 256), f32),
            pltpu.VMEM((WIDE, TR, 256), f32),
            dma((N,)),
            dma((N,)),
            dma((N,)),
            dma((N + 1,)),
            dma((N + 1,)),
            dma((N + 1,)),
            dma((N + 1,)),
            dma((N,)),
            dma((N,)),
            dma((N,)),
            dma((2,)),
            dma((2,)),
            dma,
            dma,
            dma,
        ],
        compiler_params=pltpu.CompilerParams(collective_id=collective_id, has_side_effects=True),
    )(shift_depth, sub_cell, gravity_kick, collision, density)


def branch_kernel(depth, branch):
    _, counts, places = places_of(depth)
    need = jnp.int32(0)
    for i in range(NVX):
        for j in range(i):
            gap = places[i] - places[j]
            together = jnp.logical_or(gap == 8, gap == -8)
            need = jnp.maximum(need, jnp.where(together, counts[i] + counts[j], 0))
    k = jnp.int32(0)
    for rows in LENGTHS[:-1]:
        k = k + (need > rows).astype(jnp.int32)
    branch[0] = k


def per_device(density, shift_depth, sub_cell, gravity_kick, collision):
    branches = [functools.partial(step, rows, k + 1) for k, rows in enumerate(LENGTHS)]
    smem = pl.BlockSpec(memory_space=pltpu.SMEM)
    branch = pl.pallas_call(
        branch_kernel, out_shape=jax.ShapeDtypeStruct((1,), jnp.int32), in_specs=[smem], out_specs=smem
    )(shift_depth)[0]
    kicked, coef = lax.switch(branch, branches, density, shift_depth, sub_cell, gravity_kick, collision)
    keep, gain, cool, flow_x, flow_y, flow_z = (coef[j][:, :, None] for j in range(6))
    pair = jnp.arange(256, dtype=jnp.int32)
    vx = ((pair >> 4).astype(jnp.float32) - 7.5) * STEP_XY
    vy = ((pair & 15).astype(jnp.float32) - 7.5) * STEP_XY
    level = lax.axis_index(VZ) * PLANES + jnp.arange(PLANES, dtype=jnp.int32)
    vz = ((level.astype(jnp.float32) - 11.5) * STEP_Z)[:, None, None, None]
    flat = (vx - flow_x) ** 2 + (vy - flow_y) ** 2
    return keep * kicked + gain * jnp.exp(cool * (flat + (vz - flow_z) ** 2))


def solution(mesh):
    torus = Mesh(mesh.devices.reshape(mesh.shape["gx"] // 8, 2, 4, 4, 2), AXES)
    return jax.shard_map(
        per_device,
        mesh=torus,
        in_specs=(P(VZ, GX, None, None), P(), P(), P(GX, None), P(GX, None)),
        out_specs=P(VZ, GX, None, None),
        check_vma=False,
    )
```
